128 devices in a mesh: depth: 8 (over x, core), rows: 16 (over z, y).
Axes of the slice: x: 4, y: 4, z: 4, core: 2. Of those that a mesh axis runs over, the one named last changes fastest.
Arguments:
- volume: bfloat16 [4, 128, 512, 4096], P(None, 'depth', 'rows')
- shear_rows: int32 [128], P('depth'), may hold values from -8 to 8, as said below
- shear_cols: int32 [128], P('depth'), may hold values from -8 to 8, as said below
- warp_cols: int32 [512], replicated, may hold values from -8 to 8, as said below
- warp_rows: int32 [4096], P('depth'), may hold values from -8 to 8, as said below
Outputs:
- final_image: float32 [4, 512, 4096], P(None, 'rows', 'depth')
The draws below stay inside these ranges and needn't reach their ends.
Inputs may be any that keep to these rules, and one draw needn't show every extreme that they name: `shear_rows`: both -8 and 8 occur. `shear_cols`: both -8 and 8 occur. `warp_cols`: both -8 and 8 occur. `warp_rows`: both -8 and 8 occur.
All inputs are finite; a program needn't handle non-finite values.
Results may differ from the reference program's by a relative error of at most 0.0017.
Values may be sent and summed in bfloat16 or wider, within the bound.
No kernel may reach another device: no remote copies, remote signals or barrier semaphores. Data moves between devices by JAX's collectives and lax.ppermute only.
A program may use at most 192 MiB of HBM per device.

```python
import jax
import jax.numpy as jnp
from jax import lax

X = 4096
SHIFT = 8
Z = 128
Y = 512


def draw_offsets(key, count):
    first_key, second_key, third_key = jax.random.split(key, 3)
    values = jax.random.randint(first_key, (count,), -SHIFT, SHIFT + 1)
    high_spot = jax.random.randint(second_key, (), 0, count)
    low_spot = (high_spot + 1 + jax.random.randint(third_key, (), 0, count - 1)) % count
    values = values.at[high_spot].set(SHIFT)
    values = values.at[low_spot].set(-SHIFT)
    return values.astype(jnp.int32)


def draw_volume(key, part):
    colour_key, opacity_key = jax.random.split(jax.random.fold_in(key, 11))
    colour = jax.random.uniform(colour_key, (3, Z, Y, X), jnp.float32, 0.0, 2.0)
    opacity = jnp.exp(jax.random.uniform(opacity_key, (1, Z, Y, X), jnp.float32, jnp.log(0.001), jnp.log(0.06)))
    return jnp.concatenate([colour, opacity], 0).astype(jnp.bfloat16)


def draw_shear_rows(key, part):
    return draw_offsets(jax.random.fold_in(key, 21), Z)


def draw_shear_cols(key, part):
    return draw_offsets(jax.random.fold_in(key, 22), Z)


def draw_warp_cols(key, part):
    return draw_offsets(jax.random.fold_in(key, 23), Y)


def draw_warp_rows(key, part):
    return draw_offsets(jax.random.fold_in(key, 24), X)


def setup_inputs(seed: int = 0) -> dict:
    arg_keys = jax.random.split(jax.random.key(seed), 6)
    volume = draw_volume(jax.random.fold_in(arg_keys[5], 71), 0)
    shear_rows = draw_shear_rows(jax.random.fold_in(arg_keys[5], 71), 0)
    shear_cols = draw_shear_cols(jax.random.fold_in(arg_keys[5], 71), 0)
    warp_cols = draw_warp_cols(jax.random.fold_in(arg_keys[5], 71), 0)
    warp_rows = draw_warp_rows(jax.random.fold_in(arg_keys[5], 71), 0)
    return {"volume": volume, "shear_rows": shear_rows, "shear_cols": shear_cols, "warp_cols": warp_cols, "warp_rows": warp_rows}


def weight_of(offset):
    return jnp.where(offset == 0, 0.5, jnp.where(jnp.abs(offset) == 1, 0.25, 0.0)).astype(jnp.float32)


def over_front(front_part, back_part):
    return front_part + (1.0 - front_part[3:4]) * back_part


def premultiply(slab):
    opacity = slab[3:4]
    return jnp.concatenate([slab[:3] * opacity, opacity], 0)


def shear_slice(extended, row_shift, col_shift, band_rows, band_cols, rim_width):
    band_sum = jnp.zeros((4, band_rows, band_cols + 2 * rim_width), jnp.float32)
    for offset, factor in ((-1, 0.25), (0, 0.5), (1, 0.25)):
        start = (rim_width + row_shift + offset).astype(jnp.int32)
        band_sum = band_sum + factor * lax.dynamic_slice_in_dim(extended, start, band_rows, 1)
    sheared = jnp.zeros((4, band_rows, band_cols), jnp.float32)
    for offset, factor in ((-1, 0.25), (0, 0.5), (1, 0.25)):
        start = (rim_width + col_shift + offset).astype(jnp.int32)
        sheared = sheared + factor * lax.dynamic_slice_in_dim(band_sum, start, band_cols, 2)
    return sheared


def shift_columns(picture, shifts, band_cols, rim_width):
    result = jnp.zeros((4, picture.shape[1], band_cols), jnp.float32)
    for offset in range(-rim_width, rim_width + 1):
        kernel_col = weight_of(offset - shifts)[None, :, None]
        result = result + kernel_col * picture[:, :, rim_width + offset:rim_width + offset + band_cols]
    return result


def shift_rows(picture, shifts, band_rows, rim_width):
    result = jnp.zeros((4, band_rows, picture.shape[2]), jnp.float32)
    for offset in range(-rim_width, rim_width + 1):
        kernel_row = weight_of(offset - shifts)[None, None, :]
        result = result + kernel_row * picture[:, rim_width + offset:rim_width + offset + band_rows, :]
    return result


def reference(volume, shear_rows, shear_cols, warp_cols, warp_rows):
    rim_width = SHIFT + 1
    slices_first = jnp.moveaxis(volume, 1, 0)

    def add_slice(accumulated, pieces_in):
        slice_now, row_shift, col_shift = pieces_in
        extended = jnp.pad(premultiply(slice_now.astype(jnp.float32)), ((0, 0), (rim_width, rim_width), (rim_width, rim_width)))
        return over_front(accumulated, shear_slice(extended, row_shift, col_shift, Y, X, rim_width)), None

    start_image = jnp.zeros((4, Y, X), jnp.float32)
    intermediate, _ = lax.scan(add_slice, start_image, (slices_first, shear_rows, shear_cols))
    padded_cols = jnp.pad(intermediate, ((0, 0), (0, 0), (rim_width, rim_width)))
    across = shift_columns(padded_cols, warp_cols, X, rim_width)
    padded_rows = jnp.pad(across, ((0, 0), (rim_width, rim_width), (0, 0)))
    return shift_rows(padded_rows, warp_rows, Y, rim_width)
```

```python
import functools

import jax
import jax.numpy as jnp
from jax import lax
from jax.experimental import pallas as pl
from jax.experimental.pallas import tpu as pltpu
from jax.sharding import PartitionSpec as P

SHIFT = 8
RIM = SHIFT + 1
BLOCK = 256
EDGE = 128
VMEM_LIMIT = 60 * 1024 * 1024


def rows_from_high(shift):
    return jnp.maximum(shift + 1, 0)


def rows_from_low(shift):
    return jnp.maximum(1 - shift, 0)


def pack_kernel(shear_rows, top_ref, bottom_ref, up_ref, down_ref, up_rows, down_rows, used):
    index = pl.program_id(0)
    slots = up_ref.shape[0] * 8
    tiles = up_ref.shape[3] // 128

    @pl.when(index == 0)
    def _():
        used[0] = 0
        used[1] = 0

    def scatter(source, target, row):
        def body(tile, carry):
            lane = pl.multiple_of(tile * 128, 128)
            for channel in range(4):
                target[tile, channel, pl.ds(row, 16), :] = source[
                    channel, 0, :, pl.ds(lane, 128)
                ].astype(jnp.float32)
            return carry

        lax.fori_loop(0, tiles, body, 0)

    shift = shear_rows[index]
    up_count = rows_from_high(shift)
    down_count = rows_from_low(shift)

    @pl.when(up_count > 0)
    def _():
        scatter(top_ref, up_rows, used[0])

    @pl.when(down_count > 0)
    def _():
        scatter(bottom_ref, down_rows, slots - used[1])

    used[0] = used[0] + up_count
    used[1] = used[1] + down_count

    @pl.when(index == pl.num_programs(0) - 1)
    def _():
        def flush(group, carry):
            row = pl.multiple_of(group * 8, 8)
            for tile in range(tiles):
                lanes = slice(tile * 128, tile * 128 + 128)
                for channel in range(4):
                    up_ref[group, channel, :, lanes] = up_rows[
                        tile, channel, pl.ds(row, 8), :
                    ].astype(jnp.bfloat16)
                    down_ref[group, channel, :, lanes] = down_rows[
                        tile, channel, pl.ds(pl.multiple_of(row + 16, 8), 8), :
                    ].astype(jnp.bfloat16)
            return carry

        lax.fori_loop(0, up_ref.shape[0], flush, 0)


def pack_halo(volume, shear_rows):
    _, slices, band_rows, columns = volume.shape
    groups = -(-RIM * slices // 8)
    last = band_rows // 16 - 1
    packed = jax.ShapeDtypeStruct((groups, 4, 8, columns), jnp.bfloat16)
    whole = pl.BlockSpec((groups, 4, 8, columns), lambda i, s: (0, 0, 0, 0), pipeline_mode=pl.Buffered(1))
    return pl.pallas_call(
        pack_kernel,
        out_shape=(packed, packed),
        grid_spec=pltpu.PrefetchScalarGridSpec(
            num_scalar_prefetch=1,
            grid=(slices,),
            in_specs=[
                pl.BlockSpec((4, 1, 16, columns), lambda i, s: (0, i, 0, 0)),
                pl.BlockSpec((4, 1, 16, columns), lambda i, s: (0, i, last, 0)),
            ],
            out_specs=[whole, whole],
            scratch_shapes=[
                pltpu.VMEM((columns // 128, 4, groups * 8 + 16, 128), jnp.float32),
                pltpu.VMEM((columns // 128, 4, groups * 8 + 16, 128), jnp.float32),
                pltpu.SMEM((2,), jnp.int32),
            ],
        ),
        compiler_params=pltpu.CompilerParams(vmem_limit_bytes=VMEM_LIMIT),
    )(shear_rows, volume, volume)


def shear_kernel(
    shear_rows, shear_cols, volume_ref, low_ref, high_ref, image_ref,
    inner, rim_low, rim_high, weights, filtered, total, used,
):
    index = pl.program_id(0)
    band_rows = volume_ref.shape[2]
    columns = volume_ref.shape[3]
    blocks = columns // BLOCK
    groups = low_ref.shape[0]
    row_shift = shear_rows[index]
    col_shift = shear_cols[index]

    @pl.when(index == 0)
    def _():
        used[0] = 0
        used[1] = 0
        for part in (inner, rim_low, rim_high):
            part[:, 0:EDGE] = jnp.zeros((part.shape[0], EDGE), jnp.bfloat16)
            part[:, EDGE + columns :] = jnp.zeros((part.shape[0], EDGE), jnp.bfloat16)

        def clear(block, carry):
            start = pl.multiple_of(block * BLOCK, BLOCK)
            for channel in range(4):
                total[channel, :, pl.ds(start, BLOCK)] = jnp.full(
                    (band_rows, BLOCK), 0.0 if channel < 3 else 1.0, jnp.float32
                )
            return carry

        lax.fori_loop(0, blocks, clear, 0)

    high_count = rows_from_high(row_shift)
    low_count = rows_from_low(row_shift)
    high_start = used[0]
    low_start = groups * 8 - used[1] - low_count
    used[0] = used[0] + high_count
    used[1] = used[1] + low_count
    high_group = jnp.minimum(high_start // 8, groups - 2)
    low_group = jnp.minimum(low_start // 8, groups - 2)
    high_row = 16 + band_rows - (high_start - high_group * 8)
    low_row = 16 - low_count - (low_start - low_group * 8)

    source = lax.broadcasted_iota(jnp.int32, (2 * BLOCK, BLOCK), 0)
    target = lax.broadcasted_iota(jnp.int32, (2 * BLOCK, BLOCK), 1)
    distance = jnp.abs(source - target - EDGE - col_shift)
    weights[...] = jnp.where(
        distance == 0, 0.125, jnp.where(distance == 1, 0.0625, 0.0)
    ).astype(jnp.bfloat16)

    def premultiply(block, carry):
        start = pl.multiple_of(block * BLOCK, BLOCK)
        place = pl.multiple_of(start + EDGE, EDGE)
        opacity = volume_ref[3, 0, :, pl.ds(start, BLOCK)].astype(jnp.float32)
        for channel in range(4):
            value = volume_ref[channel, 0, :, pl.ds(start, BLOCK)].astype(jnp.float32)
            if channel < 3:
                value = value * opacity
            inner[pl.ds(channel * band_rows, band_rows), pl.ds(place, BLOCK)] = value.astype(
                jnp.bfloat16
            )
        return carry

    lax.fori_loop(0, blocks, premultiply, 0)

    def premultiply_rim(packed, group, rim):
        def body(block, carry):
            start = pl.multiple_of(block * BLOCK, BLOCK)
            place = pl.multiple_of(start + EDGE, EDGE)

            def rows_of(channel):
                return jnp.concatenate(
                    [packed[group + half, channel, :, pl.ds(start, BLOCK)].astype(jnp.float32) for half in range(2)], 0
                )

            opacity = rows_of(3)
            for channel in range(4):
                value = rows_of(channel) * opacity if channel < 3 else opacity
                rim[pl.ds(channel * 16, 16), pl.ds(place, BLOCK)] = value.astype(jnp.bfloat16)
            return carry

        lax.fori_loop(0, blocks, body, 0)

    @pl.when(low_count > 0)
    def _():
        premultiply_rim(low_ref, low_group, rim_low)

    @pl.when(high_count > 0)
    def _():
        premultiply_rim(high_ref, high_group, rim_high)

    def filter_columns(part, start):
        return jnp.dot(
            part[:, pl.ds(start, 2 * BLOCK)], weights[...], preferred_element_type=jnp.float32
        )

    def composite(block, carry):
        start = pl.multiple_of(block * BLOCK, BLOCK)

        @pl.when(low_count > 0)
        def _():
            rows = filter_columns(rim_low, start)
            for channel in range(4):
                for tile in range(BLOCK // 128):
                    filtered[tile, channel, pl.ds(low_row, 16), :] = rows[
                        channel * 16 : channel * 16 + 16, tile * 128 : tile * 128 + 128
                    ]

        @pl.when(high_count > 0)
        def _():
            rows = filter_columns(rim_high, start)
            for channel in range(4):
                for tile in range(BLOCK // 128):
                    filtered[tile, channel, pl.ds(high_row, 16), :] = rows[
                        channel * 16 : channel * 16 + 16, tile * 128 : tile * 128 + 128
                    ]

        rows = filter_columns(inner, start)
        for channel in range(4):
            for tile in range(BLOCK // 128):
                filtered[tile, channel, 16 : 16 + band_rows, :] = rows[
                    channel * band_rows : (channel + 1) * band_rows, tile * 128 : tile * 128 + 128
                ]
        for tile in range(BLOCK // 128):
            lanes = pl.ds(pl.multiple_of(start + tile * 128, 128), 128)

            def sheared(channel):
                first, middle, last = (
                    filtered[tile, channel, pl.ds(16 + row_shift + offset, band_rows), :]
                    for offset in (-1, 0, 1)
                )
                return first + last + (middle + middle)

            passed = total[3, :, lanes]
            for channel in range(3):
                total[channel, :, lanes] = total[channel, :, lanes] + passed * sheared(channel)
            total[3, :, lanes] = passed - passed * sheared(3)
        return carry

    lax.fori_loop(0, blocks, composite, 0)

    @pl.when(index == pl.num_programs(0) - 1)
    def _():
        tiles = image_ref.shape[0]
        width = columns // tiles
        lane = lax.broadcasted_iota(jnp.int32, (band_rows, EDGE), 1)
        zero = jnp.zeros((band_rows, EDGE), jnp.float32)
        for channel in range(4):

            def value(start, size):
                part = total[channel, :, pl.ds(start, size)]
                return part if channel < 3 else 1.0 - part

            for tile in range(tiles):
                first = tile * width
                image_ref[tile, channel, :, 0:width] = value(first, width).astype(jnp.bfloat16)
                before = value(first - EDGE, EDGE) if tile > 0 else zero
                after = value(first + width, EDGE) if tile < tiles - 1 else zero
                image_ref[tile, channel, :, width:] = jnp.where(
                    lane < EDGE // 2, after, before
                ).astype(jnp.bfloat16)


def shear_slab(volume, shear_rows, shear_cols, low, high, tiles):
    _, slices, band_rows, columns = volume.shape
    groups = low.shape[0]
    whole = pl.BlockSpec((groups, 4, 8, columns), lambda i, a, b: (0, 0, 0, 0), pipeline_mode=pl.Buffered(1))
    image = (tiles, 4, band_rows, columns // tiles + EDGE)
    return pl.pallas_call(
        shear_kernel,
        out_shape=jax.ShapeDtypeStruct(image, jnp.bfloat16),
        grid_spec=pltpu.PrefetchScalarGridSpec(
            num_scalar_prefetch=2,
            grid=(slices,),
            in_specs=[
                pl.BlockSpec((4, 1, band_rows, columns), lambda i, a, b: (0, i, 0, 0)),
                whole,
                whole,
            ],
            out_specs=pl.BlockSpec(image, lambda i, a, b: (0, 0, 0, 0), pipeline_mode=pl.Buffered(1)),
            scratch_shapes=[
                pltpu.VMEM((4 * band_rows, columns + 2 * EDGE), jnp.bfloat16),
                pltpu.VMEM((64, columns + 2 * EDGE), jnp.bfloat16),
                pltpu.VMEM((64, columns + 2 * EDGE), jnp.bfloat16),
                pltpu.VMEM((2 * BLOCK, BLOCK), jnp.bfloat16),
                pltpu.VMEM((BLOCK // 128, 4, band_rows + 32, 128), jnp.float32),
                pltpu.VMEM((4, band_rows, columns), jnp.float32),
                pltpu.SMEM((2,), jnp.int32),
            ],
        ),
        compiler_params=pltpu.CompilerParams(vmem_limit_bytes=VMEM_LIMIT),
    )(shear_rows, shear_cols, volume, low, high)


def weight_of(offset):
    return jnp.where(offset == 0, 0.5, jnp.where(jnp.abs(offset) == 1, 0.25, 0.0))


def across_kernel(pieces_ref, shifts_ref, across_ref, top_ref, bottom_ref):
    tiles, _, band_rows, padded = pieces_ref.shape
    width = across_ref.shape[2]
    for row in range(0, band_rows, 8):
        rows = slice(row, row + 8)
        totals = [None] * 4
        passed = None
        for tile in range(tiles):
            parts = [pieces_ref[tile, channel, rows, :].astype(jnp.float32) for channel in range(4)]
            if tile == 0:
                totals = parts[:3]
                passed = 1.0 - parts[3]
            else:
                totals = [total + passed * part for total, part in zip(totals, parts[:3])]
                passed = passed - passed * parts[3]
        totals = totals[:3] + [1.0 - passed]
        shifts = jnp.broadcast_to(shifts_ref[rows, :], (8, width))
        results = [jnp.zeros((8, width), jnp.float32)] * 4
        for offset in range(-RIM, RIM + 1):
            factor = weight_of(offset - shifts)
            for channel in range(4):
                moved = pltpu.roll(totals[channel], (-offset) % padded, 1)[:, :width]
                results[channel] = results[channel] + factor * moved
        for channel in range(4):
            across_ref[channel, rows, :] = results[channel]
    for channel in range(4):
        top_ref[channel * RIM : (channel + 1) * RIM, :] = across_ref[channel, 0:RIM, :]
        bottom_ref[channel * RIM : (channel + 1) * RIM, :] = across_ref[
            channel, band_rows - RIM : band_rows, :
        ]


def warp_columns(pieces, shifts, width):
    _, _, band_rows, _ = pieces.shape
    rim = jax.ShapeDtypeStruct((4 * RIM, width), jnp.float32)
    return pl.pallas_call(
        across_kernel,
        out_shape=(jax.ShapeDtypeStruct((4, band_rows, width), jnp.float32), rim, rim),
        compiler_params=pltpu.CompilerParams(vmem_limit_bytes=VMEM_LIMIT),
    )(pieces, shifts)


def final_kernel(across_ref, low_ref, high_ref, shifts_ref, final_ref, extended):
    _, band_rows, width = across_ref.shape
    for channel in range(4):
        extended[channel, 16 : 16 + band_rows, :] = across_ref[channel]
        rim = slice(channel * RIM, (channel + 1) * RIM)
        extended[channel, 16 - RIM : 16, :] = low_ref[rim, :]
        extended[channel, 16 + band_rows : 16 + band_rows + RIM, :] = high_ref[rim, :]
    for lane in range(0, width, 128):
        lanes = slice(lane, lane + 128)
        shifts = jnp.broadcast_to(shifts_ref[:, lanes], (8, 128))
        factors = [weight_of(offset - shifts) for offset in range(-RIM, RIM + 1)]
        for channel in range(4):
            for row in range(0, band_rows, 8):
                result = jnp.zeros((8, 128), jnp.float32)
                for offset in range(-RIM, RIM + 1):
                    start = 16 + row + offset
                    result = result + factors[offset + RIM] * extended[
                        channel, start : start + 8, lanes
                    ]
                final_ref[channel, row : row + 8, lanes] = result


def warp_rows_of(across, low, high, shifts):
    _, band_rows, width = across.shape
    return pl.pallas_call(
        final_kernel,
        out_shape=jax.ShapeDtypeStruct(across.shape, jnp.float32),
        scratch_shapes=[pltpu.VMEM((4, band_rows + 32, width), jnp.float32)],
        compiler_params=pltpu.CompilerParams(vmem_limit_bytes=VMEM_LIMIT),
    )(across, low, high, shifts)


def neighbours(axis):
    count = lax.axis_size(axis)
    forward = [(i, i + 1) for i in range(count - 1)]
    return forward, [(target, source) for source, target in forward]


def per_device(volume, shear_rows, shear_cols, warp_cols, warp_rows):
    band_rows = volume.shape[2]
    columns = volume.shape[3]
    tiles = lax.axis_size("depth")
    width = columns // tiles
    forward, backward = neighbours("rows")
    up, down = pack_halo(volume, shear_rows)
    high = lax.ppermute(up, "rows", backward)
    low = lax.ppermute(down, "rows", forward)
    image = shear_slab(volume, shear_rows, shear_cols, low, high, tiles)
    pieces = lax.all_to_all(image, "depth", 0, 0, tiled=True)
    row_start = lax.axis_index("rows") * band_rows
    row_shifts = lax.dynamic_slice_in_dim(warp_cols, row_start, band_rows, 0)
    across, top, bottom = warp_columns(pieces, row_shifts[:, None], width)
    below = lax.ppermute(bottom, "rows", forward)
    above = lax.ppermute(top, "rows", backward)
    return warp_rows_of(across, below, above, warp_rows[None, :])


def solution(mesh):
    return jax.shard_map(
        per_device,
        mesh=mesh,
        in_specs=(P(None, "depth", "rows", None), P("depth"), P("depth"), P(), P("depth")),
        out_specs=P(None, "rows", "depth"),
        check_vma=False,
    )
```

```python
import functools

import jax
import jax.numpy as jnp
from jax import lax
from jax.experimental import pallas as pl
from jax.experimental.pallas import tpu as pltpu
from jax.sharding import PartitionSpec as P

SHIFT = 8
RIM = SHIFT + 1
BLOCK = 256
GROUP = 16
UNROLL = 1
LEAST = 4
STEP = 2
EDGE = 128
VMEM_LIMIT = 60 * 1024 * 1024


def rows_from_high(shift):
    return jnp.maximum(shift + 1, 0)


def rows_from_low(shift):
    return jnp.maximum(1 - shift, 0)


def pack_kernel(shear_rows, top_ref, bottom_ref, up_ref, down_ref, up_rows, down_rows, used):
    index = pl.program_id(0)
    slots = up_ref.shape[0] * 8
    tiles = up_ref.shape[3] // 128

    @pl.when(index == 0)
    def _():
        used[0] = 0
        used[1] = 0

    def scatter(source, target, row):
        def body(tile, carry):
            lane = pl.multiple_of(tile * 128, 128)
            for channel in range(4):
                target[tile, channel, pl.ds(row, 16), :] = source[
                    channel, 0, :, pl.ds(lane, 128)
                ].astype(jnp.float32)
            return carry

        lax.fori_loop(0, tiles, body, 0)

    shift = shear_rows[index]
    up_count = rows_from_high(shift)
    down_count = rows_from_low(shift)

    @pl.when(up_count > 0)
    def _():
        scatter(top_ref, up_rows, used[0])

    @pl.when(down_count > 0)
    def _():
        scatter(bottom_ref, down_rows, slots - used[1])

    used[0] = used[0] + up_count
    used[1] = used[1] + down_count

    @pl.when(index == pl.num_programs(0) - 1)
    def _():
        def flush(group, carry):
            row = pl.multiple_of(group * 8, 8)
            for tile in range(tiles):
                lanes = slice(tile * 128, tile * 128 + 128)
                for channel in range(4):
                    up_ref[group, channel, :, lanes] = up_rows[
                        tile, channel, pl.ds(row, 8), :
                    ].astype(jnp.bfloat16)
                    down_ref[group, channel, :, lanes] = down_rows[
                        tile, channel, pl.ds(pl.multiple_of(row + 16, 8), 8), :
                    ].astype(jnp.bfloat16)
            return carry

        lax.fori_loop(0, up_ref.shape[0], flush, 0)


def pack_halo(volume, shear_rows):
    _, slices, band_rows, columns = volume.shape
    groups = -(-RIM * slices // 8)
    last = band_rows // 16 - 1
    packed = jax.ShapeDtypeStruct((groups, 4, 8, columns), jnp.bfloat16)
    whole = pl.BlockSpec((groups, 4, 8, columns), lambda i, s: (0, 0, 0, 0), pipeline_mode=pl.Buffered(1))
    return pl.pallas_call(
        pack_kernel,
        out_shape=(packed, packed),
        grid_spec=pltpu.PrefetchScalarGridSpec(
            num_scalar_prefetch=1,
            grid=(slices,),
            in_specs=[
                pl.BlockSpec((4, 1, 16, columns), lambda i, s: (0, i, 0, 0)),
                pl.BlockSpec((4, 1, 16, columns), lambda i, s: (0, i, last, 0)),
            ],
            out_specs=[whole, whole],
            scratch_shapes=[
                pltpu.VMEM((columns // 128, 4, groups * 8 + 16, 128), jnp.float32),
                pltpu.VMEM((columns // 128, 4, groups * 8 + 16, 128), jnp.float32),
                pltpu.SMEM((2,), jnp.int32),
            ],
        ),
        compiler_params=pltpu.CompilerParams(vmem_limit_bytes=VMEM_LIMIT),
    )(shear_rows, volume, volume)


def shear_kernel(
    shear_rows, shear_cols, volume_ref, low_ref, high_ref, image_ref,
    inner, rim, weights, filtered, total, used,
):
    index = pl.program_id(0)
    band_rows = volume_ref.shape[2]
    columns = volume_ref.shape[3]
    blocks = columns // BLOCK
    groups = low_ref.shape[0]
    row_shift = shear_rows[index]
    col_shift = shear_cols[index]

    @pl.when(index == 0)
    def _():
        used[0] = 0
        used[1] = 0
        for part in (inner, rim):
            none = jnp.zeros((part.shape[1], EDGE), jnp.bfloat16)
            part[0, :, 0:EDGE] = none
            part[blocks, :, EDGE:] = none

        def clear(block, carry):
            start = pl.multiple_of(block * BLOCK, BLOCK)
            for channel in range(4):
                total[channel, :, pl.ds(start, BLOCK)] = jnp.full(
                    (band_rows, BLOCK), 0.0 if channel < 3 else 1.0, jnp.float32
                )
            return carry

        lax.fori_loop(0, blocks, clear, 0)

    high_count = rows_from_high(row_shift)
    low_count = rows_from_low(row_shift)
    high_start = used[0]
    low_start = groups * 8 - used[1] - low_count
    used[0] = used[0] + high_count
    used[1] = used[1] + low_count
    high_group = jnp.minimum(high_start // 8, groups - 2)
    low_group = jnp.minimum(low_start // 8, groups - 2)
    high_row = 16 + band_rows - (high_start - high_group * 8)
    low_row = 16 - low_count - (low_start - low_group * 8)

    source = lax.broadcasted_iota(jnp.int32, (2 * BLOCK, BLOCK), 0)
    target = lax.broadcasted_iota(jnp.int32, (2 * BLOCK, BLOCK), 1)
    distance = jnp.abs(source - target - EDGE - col_shift)
    weights[...] = jnp.where(
        distance == 0, 0.125, jnp.where(distance == 1, 0.0625, 0.0)
    ).astype(jnp.bfloat16)

    def premultiply(load, part, count):
        def rows_at(block, lanes, start, size):
            opacity = load(3, start, size)
            for channel in range(4):
                value = load(channel, start, size)
                if channel < 3:
                    value = value * opacity
                part[block, channel * count : (channel + 1) * count, lanes] = value.astype(
                    jnp.bfloat16
                )

        def body(block, carry):
            start = pl.multiple_of(block * BLOCK - EDGE, EDGE)
            rows_at(block, slice(0, BLOCK), start, BLOCK)
            return carry

        rows_at(0, slice(EDGE, BLOCK), 0, EDGE)
        rows_at(blocks, slice(0, EDGE), columns - EDGE, EDGE)
        lax.fori_loop(1, blocks, body, 0)

    def filter_columns(part, count, row):
        def body(step, carry):
            first = step * GROUP
            lhs0 = part[pl.ds(first, GROUP)].reshape(GROUP * 4 * count, BLOCK)
            lhs1 = part[pl.ds(first + 1, GROUP)].reshape(GROUP * 4 * count, BLOCK)
            rows = jnp.dot(
                lhs0, weights[0:BLOCK, :], preferred_element_type=jnp.float32
            ) + jnp.dot(lhs1, weights[BLOCK:, :], preferred_element_type=jnp.float32)
            for block in range(GROUP):
                for channel in range(4):
                    top = (block * 4 + channel) * count
                    for half in range(2):
                        filtered[(first + block) * 2 + half, channel, pl.ds(row, count), :] = rows[
                            top : top + count, half * 128 : half * 128 + 128
                        ]
            return carry

        lax.fori_loop(0, blocks // GROUP, body, 0)

    def rim_of(packed, group, row):
        def load(channel, start, size):
            return jnp.concatenate(
                [
                    packed[group + half, channel, :, pl.ds(start, size)].astype(jnp.float32)
                    for half in range(2)
                ],
                0,
            )

        premultiply(load, rim, 16)
        filter_columns(rim, 16, row)

    @pl.when(low_count > 0)
    def _():
        rim_of(low_ref, low_group, low_row)

    @pl.when(high_count > 0)
    def _():
        rim_of(high_ref, high_group, high_row)

    premultiply(
        lambda channel, start, size: volume_ref[channel, 0, :, pl.ds(start, size)].astype(
            jnp.float32
        ),
        inner,
        band_rows,
    )
    filter_columns(inner, band_rows, 16)

    def composite(tile, carry):
        lanes = pl.ds(pl.multiple_of(tile * 128, 128), 128)

        def sheared(channel):
            first, middle, last = (
                filtered[tile, channel, pl.ds(16 + row_shift + offset, band_rows), :]
                for offset in (-1, 0, 1)
            )
            return first + last + (middle + middle)

        passed = total[3, :, lanes]
        for channel in range(3):
            total[channel, :, lanes] = total[channel, :, lanes] + passed * sheared(channel)
        total[3, :, lanes] = passed - passed * sheared(3)
        return carry

    lax.fori_loop(0, columns // 128, composite, 0, unroll=UNROLL)

    @pl.when(index == pl.num_programs(0) - 1)
    def _():
        tiles = image_ref.shape[0]
        width = columns // tiles
        lane = lax.broadcasted_iota(jnp.int32, (band_rows, EDGE), 1)
        zero = jnp.zeros((band_rows, EDGE), jnp.float32)
        for channel in range(4):

            def value(start, size):
                part = total[channel, :, pl.ds(start, size)]
                return part if channel < 3 else 1.0 - part

            for tile in range(tiles):
                first = tile * width
                image_ref[tile, channel, :, 0:width] = value(first, width).astype(jnp.bfloat16)
                before = value(first - EDGE, EDGE) if tile > 0 else zero
                after = value(first + width, EDGE) if tile < tiles - 1 else zero
                image_ref[tile, channel, :, width:] = jnp.where(
                    lane < EDGE // 2, after, before
                ).astype(jnp.bfloat16)


def shear_slab(volume, shear_rows, shear_cols, low, high, tiles):
    _, slices, band_rows, columns = volume.shape
    groups = low.shape[0]
    whole = pl.BlockSpec((groups, 4, 8, columns), lambda i, a, b: (0, 0, 0, 0), pipeline_mode=pl.Buffered(1))
    image = (tiles, 4, band_rows, columns // tiles + EDGE)
    return pl.pallas_call(
        shear_kernel,
        out_shape=jax.ShapeDtypeStruct(image, jnp.bfloat16),
        grid_spec=pltpu.PrefetchScalarGridSpec(
            num_scalar_prefetch=2,
            grid=(slices,),
            in_specs=[
                pl.BlockSpec((4, 1, band_rows, columns), lambda i, a, b: (0, i, 0, 0)),
                whole,
                whole,
            ],
            out_specs=pl.BlockSpec(image, lambda i, a, b: (0, 0, 0, 0), pipeline_mode=pl.Buffered(1)),
            scratch_shapes=[
                pltpu.VMEM((columns // BLOCK + 1, 4 * band_rows, BLOCK), jnp.bfloat16),
                pltpu.VMEM((columns // BLOCK + 1, 64, BLOCK), jnp.bfloat16),
                pltpu.VMEM((2 * BLOCK, BLOCK), jnp.bfloat16),
                pltpu.VMEM((columns // 128, 4, band_rows + 32, 128), jnp.float32),
                pltpu.VMEM((4, band_rows, columns), jnp.float32),
                pltpu.SMEM((2,), jnp.int32),
            ],
        ),
        compiler_params=pltpu.CompilerParams(vmem_limit_bytes=VMEM_LIMIT),
    )(shear_rows, shear_cols, volume, low, high)


def weight_of(offset):
    return jnp.where(offset == 0, 0.5, jnp.where(jnp.abs(offset) == 1, 0.25, 0.0))


def across_kernel(pieces_ref, shifts_ref, across_ref, top_ref, bottom_ref):
    tiles, _, band_rows, padded = pieces_ref.shape
    width = across_ref.shape[2]
    for row in range(0, band_rows, 8):
        rows = slice(row, row + 8)
        totals = [None] * 4
        passed = None
        for tile in range(tiles):
            parts = [pieces_ref[tile, channel, rows, :].astype(jnp.float32) for channel in range(4)]
            if tile == 0:
                totals = parts[:3]
                passed = 1.0 - parts[3]
            else:
                totals = [total + passed * part for total, part in zip(totals, parts[:3])]
                passed = passed - passed * parts[3]
        totals = totals[:3] + [1.0 - passed]
        shifts = jnp.broadcast_to(shifts_ref[rows, :], (8, width))
        results = [jnp.zeros((8, width), jnp.float32)] * 4
        for offset in range(-RIM, RIM + 1):
            factor = weight_of(offset - shifts)
            for channel in range(4):
                moved = pltpu.roll(totals[channel], (-offset) % padded, 1)[:, :width]
                results[channel] = results[channel] + factor * moved
        for channel in range(4):
            across_ref[channel, rows, :] = results[channel]
    for channel in range(4):
        top_ref[channel * RIM : (channel + 1) * RIM, :] = across_ref[channel, 0:RIM, :]
        bottom_ref[channel * RIM : (channel + 1) * RIM, :] = across_ref[
            channel, band_rows - RIM : band_rows, :
        ]


def warp_columns(pieces, shifts, width):
    _, _, band_rows, _ = pieces.shape
    rim = jax.ShapeDtypeStruct((4 * RIM, width), jnp.float32)
    return pl.pallas_call(
        across_kernel,
        out_shape=(jax.ShapeDtypeStruct((4, band_rows, width), jnp.float32), rim, rim),
        compiler_params=pltpu.CompilerParams(vmem_limit_bytes=VMEM_LIMIT),
    )(pieces, shifts)


def final_kernel(across_ref, low_ref, high_ref, shifts_ref, final_ref, extended):
    _, band_rows, width = across_ref.shape
    for channel in range(4):
        extended[channel, 16 : 16 + band_rows, :] = across_ref[channel]
        rim = slice(channel * RIM, (channel + 1) * RIM)
        extended[channel, 16 - RIM : 16, :] = low_ref[rim, :]
        extended[channel, 16 + band_rows : 16 + band_rows + RIM, :] = high_ref[rim, :]
    for lane in range(0, width, 128):
        lanes = slice(lane, lane + 128)
        shifts = jnp.broadcast_to(shifts_ref[:, lanes], (8, 128))
        factors = [weight_of(offset - shifts) for offset in range(-RIM, RIM + 1)]
        for channel in range(4):
            for row in range(0, band_rows, 8):
                result = jnp.zeros((8, 128), jnp.float32)
                for offset in range(-RIM, RIM + 1):
                    start = 16 + row + offset
                    result = result + factors[offset + RIM] * extended[
                        channel, start : start + 8, lanes
                    ]
                final_ref[channel, row : row + 8, lanes] = result


def warp_rows_of(across, low, high, shifts):
    _, band_rows, width = across.shape
    return pl.pallas_call(
        final_kernel,
        out_shape=jax.ShapeDtypeStruct(across.shape, jnp.float32),
        scratch_shapes=[pltpu.VMEM((4, band_rows + 32, width), jnp.float32)],
        compiler_params=pltpu.CompilerParams(vmem_limit_bytes=VMEM_LIMIT),
    )(across, low, high, shifts)


def neighbours(axis):
    count = lax.axis_size(axis)
    forward = [(i, i + 1) for i in range(count - 1)]
    return forward, [(target, source) for source, target in forward]


def per_device(volume, shear_rows, shear_cols, warp_cols, warp_rows):
    band_rows = volume.shape[2]
    columns = volume.shape[3]
    tiles = lax.axis_size("depth")
    width = columns // tiles
    forward, backward = neighbours("rows")
    up, down = pack_halo(volume, shear_rows)
    most = up.shape[0]
    needed = jnp.maximum(
        jnp.sum(rows_from_high(shear_rows)), jnp.sum(rows_from_low(shear_rows))
    )
    sizes = list(range(LEAST, most, STEP)) + [most]

    def with_groups(groups):
        def branch(up, down, volume, shear_rows, shear_cols):
            high = lax.ppermute(up[:groups], "rows", backward)
            low = lax.ppermute(down[most - groups :], "rows", forward)
            return shear_slab(volume, shear_rows, shear_cols, low, high, tiles)

        return branch

    choice = jnp.clip((needed + (STEP * 8 - 1) - LEAST * 8) // (STEP * 8), 0, len(sizes) - 1)
    image = lax.switch(
        choice, [with_groups(groups) for groups in sizes], up, down, volume, shear_rows, shear_cols
    )
    pieces = lax.all_to_all(image, "depth", 0, 0, tiled=True)
    row_start = lax.axis_index("rows") * band_rows
    row_shifts = lax.dynamic_slice_in_dim(warp_cols, row_start, band_rows, 0)
    across, top, bottom = warp_columns(pieces, row_shifts[:, None], width)
    below = lax.ppermute(bottom, "rows", forward)
    above = lax.ppermute(top, "rows", backward)
    return warp_rows_of(across, below, above, warp_rows[None, :])


def solution(mesh):
    return jax.shard_map(
        per_device,
        mesh=mesh,
        in_specs=(P(None, "depth", "rows", None), P("depth"), P("depth"), P(), P("depth")),
        out_specs=P(None, "rows", "depth"),
        check_vma=False,
    )
```

```python
import functools

import jax
import jax.numpy as jnp
from jax import lax
from jax.experimental import pallas as pl
from jax.experimental.pallas import tpu as pltpu
from jax.sharding import PartitionSpec as P

SHIFT = 8
RIM = SHIFT + 1
BLOCK = 256
GROUP = 16
UNROLL = 2
PACK_UNROLL = 8
SIZES = (6, 7, 8, 9, 11)
ORDERED = False
EDGE = 128
VMEM_LIMIT = 60 * 1024 * 1024


def rows_from_high(shift):
    return jnp.maximum(shift + 1, 0)


def rows_from_low(shift):
    return jnp.maximum(1 - shift, 0)


def pack_kernel(
    shear_rows, volume_ref, up_first, up_second, down_first, down_second,
    up_tiles, down_tiles, up_rows, down_rows, up_out, down_out, in_sems, out_sems,
):
    early = up_first.shape[0]
    late = up_second.shape[0]
    groups = early + late
    slices = volume_ref.shape[1]
    band_rows = volume_ref.shape[2]
    tiles = up_first.shape[3] // 128

    def fetch(index, side, count, act):
        buffer = (up_tiles, down_tiles)[side]
        first = 0 if side == 0 else band_rows - count
        place = 0 if side == 0 else 16 - count
        copy = pltpu.make_async_copy(
            volume_ref.at[:, index, pl.ds(first, count), :],
            buffer.at[index, :, pl.ds(place, count), :],
            in_sems.at[side, index],
        )
        act(copy)

    def each_size(needed, act):
        @pl.when((needed > 0) & (needed <= 8))
        def _():
            act(8)

        @pl.when(needed > 8)
        def _():
            act(16)

    def start_slice(index, carry):
        shift = shear_rows[index]
        each_size(rows_from_high(shift), lambda n: fetch(index, 0, n, lambda c: c.start()))
        each_size(rows_from_low(shift), lambda n: fetch(index, 1, n, lambda c: c.start()))
        return carry

    lax.fori_loop(0, slices, start_slice, 0)

    def scatter(index, side, count, row):
        fetch(index, side, count, lambda c: c.wait())
        source = (up_tiles, down_tiles)[side]
        target = (up_rows, down_rows)[side]
        first = 0 if side == 0 else 16 - count

        def body(tile, carry):
            lane = pl.multiple_of(tile * 128, 128)
            for channel in range(4):
                target[tile, channel, pl.ds(row, count), :] = source[
                    index, channel, first : first + count, pl.ds(lane, 128)
                ].astype(jnp.float32)
            return carry

        lax.fori_loop(0, tiles, body, 0, unroll=PACK_UNROLL)

    def pack_slice(index, used):
        up_used, down_used = used
        shift = shear_rows[index]
        up_count = rows_from_high(shift)
        down_count = rows_from_low(shift)
        down_stop = groups * 8 + 16 - down_used
        each_size(up_count, lambda n: scatter(index, 0, n, up_used))
        each_size(down_count, lambda n: scatter(index, 1, n, down_stop - n))
        return up_used + up_count, down_used + down_count

    lax.fori_loop(0, slices, pack_slice, (0, 0))

    def flush(group, side):
        source = (up_rows, down_rows)[side]
        target = (up_out, down_out)[side]

        def body(tile, carry):
            lanes = pl.ds(pl.multiple_of(tile * 128, 128), 128)
            row = pl.multiple_of(group * 8 + 16 * side, 8)
            for channel in range(4):
                target[group, channel, :, lanes] = source[tile, channel, pl.ds(row, 8), :].astype(
                    jnp.bfloat16
                )
            return carry

        lax.fori_loop(0, tiles, body, 0, unroll=PACK_UNROLL)

    chunks = (
        (up_first, 0, 0, early),
        (down_first, 1, late, early),
        (up_second, 0, early, late),
        (down_second, 1, 0, late),
    )

    def send(target, side, group, first):
        source = (up_out, down_out)[side]
        return pltpu.make_async_copy(
            source.at[group], target.at[group - first], out_sems.at[side, group]
        )

    for target, side, first, count in chunks:

        def start(group, carry):
            flush(group, side)
            send(target, side, group, first).start()
            return carry

        lax.fori_loop(first, first + count, start, 0)
    for target, side, first, count in chunks:

        def finish(group, carry):
            send(target, side, group, first).wait()
            return carry

        lax.fori_loop(first, first + count, finish, 0)


def pack_halo(volume, shear_rows, early, late):
    _, slices, _, columns = volume.shape
    groups = early + late

    def packed(count):
        return jax.ShapeDtypeStruct((count, 4, 8, columns), jnp.bfloat16)

    tiles = pltpu.VMEM((slices, 4, 16, columns), jnp.bfloat16)
    rows = pltpu.VMEM((columns // 128, 4, groups * 8 + 16, 128), jnp.float32)
    out = pltpu.VMEM((groups, 4, 8, columns), jnp.bfloat16)
    return pl.pallas_call(
        pack_kernel,
        out_shape=(packed(early), packed(late), packed(early), packed(late)),
        grid_spec=pltpu.PrefetchScalarGridSpec(
            num_scalar_prefetch=1,
            grid=(1,),
            in_specs=[pl.BlockSpec(memory_space=pl.ANY)],
            out_specs=[pl.BlockSpec(memory_space=pl.ANY)] * 4,
            scratch_shapes=[
                tiles, tiles, rows, rows, out, out,
                pltpu.SemaphoreType.DMA((2, slices)),
                pltpu.SemaphoreType.DMA((2, groups)),
            ],
        ),
        compiler_params=pltpu.CompilerParams(vmem_limit_bytes=VMEM_LIMIT),
    )(shear_rows, volume)


def shear_kernel(part, *refs):
    shear_rows, shear_cols, bounds, volume_ref = refs[:4]
    if part == "front":
        low_refs, high_refs = [refs[4]], [refs[5]]
        before_ref, total, inner, rim, weights, filtered, halo, slabs, sems, slab_sems = None, *refs[6:]
    else:
        low_refs, high_refs = [refs[5], refs[4]], [refs[6], refs[7]]
        before_ref, image_ref, inner, rim, weights, filtered, halo, slabs, sems, slab_sems, total = refs[8:]
    begin = bounds[0]
    end = bounds[1]
    band_rows = volume_ref.shape[2]
    columns = volume_ref.shape[3]
    blocks = columns // BLOCK
    groups = halo.shape[1]
    stacked = min(GROUP, blocks)

    def fetch(index):
        slot = lax.rem(index - begin, 2)
        return pltpu.make_async_copy(volume_ref.at[:, index], slabs.at[slot], slab_sems.at[slot])

    copies = []
    for side, packed in enumerate((low_refs, high_refs)):
        first = 0
        for ref in packed:
            count = ref.shape[0]
            copies.append((ref, halo.at[side, pl.ds(first, count)]))
            first += count
    if before_ref is not None:
        copies.append((before_ref, total))
    copies = [
        pltpu.make_async_copy(source, target, sems.at[place])
        for place, (source, target) in enumerate(copies)
    ]

    fetch(begin).start()
    for copy in copies:
        copy.start()
    for edge in (inner, rim):
        none = jnp.zeros((edge.shape[1], EDGE), jnp.bfloat16)
        edge[0, :, 0:EDGE] = none
        edge[blocks, :, EDGE:] = none
    if before_ref is None:

        def clear(block, carry):
            start = pl.multiple_of(block * BLOCK, BLOCK)
            for channel in range(4):
                total[channel, :, pl.ds(start, BLOCK)] = jnp.full(
                    (band_rows, BLOCK), 0.0 if channel < 3 else 1.0, jnp.float32
                )
            return carry

        lax.fori_loop(0, blocks, clear, 0)

    def add(earlier, carry):
        shift = shear_rows[earlier]
        return carry[0] + rows_from_low(shift), carry[1] + rows_from_high(shift)

    def shear_slice(index, slot, used):
        row_shift = shear_rows[index]
        col_shift = shear_cols[index]
        low_count = rows_from_low(row_shift)
        high_count = rows_from_high(row_shift)
        low_start = groups * 8 - used[0] - low_count
        high_start = used[1]
        source = lax.broadcasted_iota(jnp.int32, (2 * BLOCK, BLOCK), 0)
        target = lax.broadcasted_iota(jnp.int32, (2 * BLOCK, BLOCK), 1)
        distance = jnp.abs(source - target - EDGE - col_shift)
        weights[...] = jnp.where(
            distance == 0, 0.125, jnp.where(distance == 1, 0.0625, 0.0)
        ).astype(jnp.bfloat16)

        def premultiply(load, part, count):
            def rows_at(block, lanes, start, size):
                opacity = load(3, start, size)
                for channel in range(4):
                    value = load(channel, start, size)
                    if channel < 3:
                        value = value * opacity
                    part[block, channel * count : (channel + 1) * count, lanes] = value.astype(
                        jnp.bfloat16
                    )

            def body(block, carry):
                start = pl.multiple_of(block * BLOCK - EDGE, EDGE)
                rows_at(block, slice(0, BLOCK), start, BLOCK)
                return carry

            rows_at(0, slice(EDGE, BLOCK), 0, EDGE)
            rows_at(blocks, slice(0, EDGE), columns - EDGE, EDGE)
            lax.fori_loop(1, blocks, body, 0, unroll=3)

        def filter_columns(part, count, row):
            def body(step, carry):
                first = step * stacked
                lhs0 = part[pl.ds(first, stacked)].reshape(stacked * 4 * count, BLOCK)
                lhs1 = part[pl.ds(first + 1, stacked)].reshape(stacked * 4 * count, BLOCK)
                rows = jnp.dot(
                    lhs0, weights[0:BLOCK, :], preferred_element_type=jnp.float32
                ) + jnp.dot(lhs1, weights[BLOCK:, :], preferred_element_type=jnp.float32)
                for block in range(stacked):
                    for channel in range(4):
                        top = (block * 4 + channel) * count
                        for half in range(2):
                            filtered[(first + block) * 2 + half, channel, pl.ds(row, count), :] = rows[
                                top : top + count, half * 128 : half * 128 + 128
                            ]
                return carry

            lax.fori_loop(0, blocks // stacked, body, 0)

        premultiply(
            lambda channel, start, size: slabs[slot, channel, :, pl.ds(start, size)].astype(
                jnp.float32
            ),
            inner,
            band_rows,
        )

        @pl.when(index == begin)
        def _():
            for copy in copies:
                copy.wait()

        def rim_of(side, carry):
            packed_row = jnp.where(side == 0, low_start, high_start)
            group = jnp.minimum(packed_row // 8, groups - 2)
            place = jnp.where(side == 0, 16 - low_count, 16 + band_rows)

            def load(channel, start, size):
                return jnp.concatenate(
                    [
                        halo[side, group + half, channel, :, pl.ds(start, size)].astype(jnp.float32)
                        for half in range(2)
                    ],
                    0,
                )

            premultiply(load, rim, 16)
            filter_columns(rim, 16, place - (packed_row - group * 8))
            return carry

        lax.fori_loop(
            jnp.where(low_count > 0, 0, 1), jnp.where(high_count > 0, 2, 1), rim_of, 0
        )
        filter_columns(inner, band_rows, 16)

        def composite(tile, carry):
            lanes = pl.ds(pl.multiple_of(tile * 128, 128), 128)

            def sheared(channel):
                first, middle, last = (
                    filtered[tile, channel, pl.ds(16 + row_shift + offset, band_rows), :]
                    for offset in (-1, 0, 1)
                )
                return first + last + (middle + middle)

            passed = total[3, :, lanes]
            for channel in range(3):
                total[channel, :, lanes] = total[channel, :, lanes] + passed * sheared(channel)
            total[3, :, lanes] = passed - passed * sheared(3)
            return carry

        lax.fori_loop(0, columns // 128, composite, 0, unroll=UNROLL)

    def one_slice(index, used):
        fetch(index).wait()

        @pl.when(index + 1 < end)
        def _():
            fetch(index + 1).start()

        shear_slice(index, lax.rem(index - begin, 2), used)
        return add(index, used)

    lax.fori_loop(begin, end, one_slice, lax.fori_loop(0, begin, add, (0, 0)))
    if part == "back":
        emit_tiles(total, image_ref)


def emit_tiles(total, image_ref):
    _, band_rows, columns = total.shape
    tiles = image_ref.shape[0]
    width = columns // tiles
    lane = lax.broadcasted_iota(jnp.int32, (band_rows, EDGE), 1)

    def value(channel, start, size):
        part = total[channel, :, pl.ds(pl.multiple_of(start, EDGE), size)]
        return part if channel < 3 else 1.0 - part

    def body(tile, carry):
        first = tile * width
        for channel in range(4):
            image_ref[tile, channel, :, 0:width] = value(channel, first, width).astype(
                jnp.bfloat16
            )
            before = value(channel, jnp.maximum(first - EDGE, 0), EDGE)
            after = value(channel, jnp.minimum(first + width, columns - EDGE), EDGE)
            before = jnp.where(tile > 0, before, 0.0)
            after = jnp.where(tile < tiles - 1, after, 0.0)
            image_ref[tile, channel, :, width:] = jnp.where(
                lane < EDGE // 2, after, before
            ).astype(jnp.bfloat16)
        return carry

    lax.fori_loop(0, tiles, body, 0)


def shear_part(part, bounds, volume, shear_rows, shear_cols, packed, before, tiles):
    _, _, band_rows, columns = volume.shape
    groups = sum(chunk.shape[0] for chunk in packed) // 2

    outside = list(packed) + ([] if before is None else [before])
    total_shape = (4, band_rows, columns)
    scratch = [
        pltpu.VMEM((columns // BLOCK + 1, 4 * band_rows, BLOCK), jnp.bfloat16),
        pltpu.VMEM((columns // BLOCK + 1, 64, BLOCK), jnp.bfloat16),
        pltpu.VMEM((2 * BLOCK, BLOCK), jnp.bfloat16),
        pltpu.VMEM((columns // 128, 4, band_rows + 32, 128), jnp.float32),
        pltpu.VMEM((2, groups, 4, 8, columns), jnp.bfloat16),
        pltpu.VMEM((2, 4, band_rows, columns), jnp.bfloat16),
        pltpu.SemaphoreType.DMA((len(outside),)),
        pltpu.SemaphoreType.DMA((2,)),
    ]
    if part == "front":
        out = jax.ShapeDtypeStruct(total_shape, jnp.float32)
    else:
        image = (tiles, 4, band_rows, columns // tiles + EDGE)
        out = jax.ShapeDtypeStruct(image, jnp.bfloat16)
        scratch.append(pltpu.VMEM(total_shape, jnp.float32))
    whole = len(out.shape)
    return pl.pallas_call(
        functools.partial(shear_kernel, part),
        out_shape=out,
        grid_spec=pltpu.PrefetchScalarGridSpec(
            num_scalar_prefetch=3,
            grid=(1,),
            in_specs=[pl.BlockSpec(memory_space=pl.ANY)] * (1 + len(outside)),
            out_specs=pl.BlockSpec(
                out.shape, lambda i, a, b, c: (0,) * whole, pipeline_mode=pl.Buffered(1)
            ),
            scratch_shapes=scratch,
        ),
        compiler_params=pltpu.CompilerParams(vmem_limit_bytes=VMEM_LIMIT),
        cost_estimate=pl.CostEstimate(
            flops=2 * 512 * volume.size, transcendentals=0, bytes_accessed=volume.size
        ),
    )(shear_rows, shear_cols, bounds, volume, *outside)


def weight_of(offset):
    return jnp.where(offset == 0, 0.5, jnp.where(jnp.abs(offset) == 1, 0.25, 0.0))


def across_kernel(pieces_ref, shifts_ref, across_ref, top_ref, bottom_ref):
    tiles, _, band_rows, padded = pieces_ref.shape
    width = across_ref.shape[2]
    for row in range(0, band_rows, 8):
        rows = slice(row, row + 8)
        totals = [None] * 4
        passed = None
        for tile in range(tiles):
            parts = [pieces_ref[tile, channel, rows, :].astype(jnp.float32) for channel in range(4)]
            if tile == 0:
                totals = parts[:3]
                passed = 1.0 - parts[3]
            else:
                totals = [total + passed * part for total, part in zip(totals, parts[:3])]
                passed = passed - passed * parts[3]
        totals = totals[:3] + [1.0 - passed]
        shifts = jnp.broadcast_to(shifts_ref[rows, :], (8, width))
        results = [jnp.zeros((8, width), jnp.float32)] * 4
        for offset in range(-RIM, RIM + 1):
            factor = weight_of(offset - shifts)
            for channel in range(4):
                moved = pltpu.roll(totals[channel], (-offset) % padded, 1)[:, :width]
                results[channel] = results[channel] + factor * moved
        for channel in range(4):
            across_ref[channel, rows, :] = results[channel]
    for channel in range(4):
        top_ref[channel * RIM : (channel + 1) * RIM, :] = across_ref[channel, 0:RIM, :]
        bottom_ref[channel * RIM : (channel + 1) * RIM, :] = across_ref[
            channel, band_rows - RIM : band_rows, :
        ]


def warp_columns(pieces, shifts, width):
    _, _, band_rows, _ = pieces.shape
    rim = jax.ShapeDtypeStruct((4 * RIM, width), jnp.float32)
    return pl.pallas_call(
        across_kernel,
        out_shape=(jax.ShapeDtypeStruct((4, band_rows, width), jnp.float32), rim, rim),
        compiler_params=pltpu.CompilerParams(vmem_limit_bytes=VMEM_LIMIT),
    )(pieces, shifts)


def final_kernel(across_ref, low_ref, high_ref, shifts_ref, final_ref, extended):
    _, band_rows, width = across_ref.shape
    for channel in range(4):
        extended[channel, 16 : 16 + band_rows, :] = across_ref[channel]
        rim = slice(channel * RIM, (channel + 1) * RIM)
        extended[channel, 16 - RIM : 16, :] = low_ref[rim, :]
        extended[channel, 16 + band_rows : 16 + band_rows + RIM, :] = high_ref[rim, :]
    for lane in range(0, width, 128):
        lanes = slice(lane, lane + 128)
        shifts = jnp.broadcast_to(shifts_ref[:, lanes], (8, 128))
        factors = [weight_of(offset - shifts) for offset in range(-RIM, RIM + 1)]
        for channel in range(4):
            for row in range(0, band_rows, 8):
                result = jnp.zeros((8, 128), jnp.float32)
                for offset in range(-RIM, RIM + 1):
                    start = 16 + row + offset
                    result = result + factors[offset + RIM] * extended[
                        channel, start : start + 8, lanes
                    ]
                final_ref[channel, row : row + 8, lanes] = result


def warp_rows_of(across, low, high, shifts):
    _, band_rows, width = across.shape
    return pl.pallas_call(
        final_kernel,
        out_shape=jax.ShapeDtypeStruct(across.shape, jnp.float32),
        scratch_shapes=[pltpu.VMEM((4, band_rows + 32, width), jnp.float32)],
        compiler_params=pltpu.CompilerParams(vmem_limit_bytes=VMEM_LIMIT),
    )(across, low, high, shifts)


def neighbours(axis):
    count = lax.axis_size(axis)
    forward = [(i, i + 1) for i in range(count - 1)]
    return forward, [(target, source) for source, target in forward]


def per_device(volume, shear_rows, shear_cols, warp_cols, warp_rows):
    band_rows = volume.shape[2]
    columns = volume.shape[3]
    tiles = lax.axis_size("depth")
    width = columns // tiles
    forward, backward = neighbours("rows")
    slices = volume.shape[1]
    most = -(-RIM * slices // 8)
    sizes = [size for size in SIZES if size < most] + [most]
    earlier = jnp.arange(slices)[None, :] <= jnp.arange(slices)[:, None]
    reach = jnp.maximum(
        jnp.sum(jnp.where(earlier, rows_from_high(shear_rows)[None, :], 0), 1),
        jnp.sum(jnp.where(earlier, rows_from_low(shear_rows)[None, :], 0), 1),
    )
    needed = reach[slices - 1]
    choice = sum((needed > 8 * size).astype(jnp.int32) for size in sizes[:-1])

    def with_groups(groups):
        early = (groups + 1) // 2
        late = groups - early

        def branch(volume, shear_rows, shear_cols, reach):
            middle = jnp.minimum(jnp.sum((reach <= 8 * early).astype(jnp.int32)), slices - 1)
            begin, end = jnp.zeros_like(middle), jnp.full_like(middle, slices)
            up_first, up_second, down_first, down_second = pack_halo(
                volume, shear_rows, early, late
            )
            high_first = lax.ppermute(up_first, "rows", backward)
            low_first = lax.ppermute(down_first, "rows", forward)
            if ORDERED:
                high_first, low_first, up_second, down_second = lax.optimization_barrier(
                    (high_first, low_first, up_second, down_second)
                )
            high_second = lax.ppermute(up_second, "rows", backward)
            low_second = lax.ppermute(down_second, "rows", forward)
            total = shear_part(
                "front", jnp.stack([begin, middle]), volume, shear_rows, shear_cols,
                (low_first, high_first), None, tiles,
            )
            return shear_part(
                "back", jnp.stack([middle, end]), volume, shear_rows, shear_cols,
                (low_first, low_second, high_first, high_second), total, tiles,
            )

        return branch

    image = lax.switch(
        choice, [with_groups(groups) for groups in sizes], volume, shear_rows, shear_cols, reach
    )
    pieces = lax.all_to_all(image, "depth", 0, 0, tiled=True)
    row_start = lax.axis_index("rows") * band_rows
    row_shifts = lax.dynamic_slice_in_dim(warp_cols, row_start, band_rows, 0)
    across, top, bottom = warp_columns(pieces, row_shifts[:, None], width)
    below = lax.ppermute(bottom, "rows", forward)
    above = lax.ppermute(top, "rows", backward)
    return warp_rows_of(across, below, above, warp_rows[None, :])


def solution(mesh):
    return jax.shard_map(
        per_device,
        mesh=mesh,
        in_specs=(P(None, "depth", "rows", None), P("depth"), P("depth"), P(), P("depth")),
        out_specs=P(None, "rows", "depth"),
        check_vma=False,
    )
```

```python
import functools

import jax
import jax.numpy as jnp
from jax import lax
from jax.experimental import pallas as pl
from jax.experimental.pallas import tpu as pltpu
from jax.sharding import PartitionSpec as P

SHIFT = 8
RIM = SHIFT + 1
BLOCK = 256
GROUP = 16
ROW_UNROLL = 3
PREMULT_UNROLL = 2
PACK_UNROLL = 8
DEPTH = 4
SIZES = (6, 7, 8, 9, 11)
ORDERED = False
EDGE = 128
VMEM_LIMIT = 60 * 1024 * 1024


def rows_from_high(shift):
    return jnp.maximum(shift + 1, 0)


def rows_from_low(shift):
    return jnp.maximum(1 - shift, 0)


def pack_kernel(
    shear_rows, volume_ref, up_first, up_second, down_first, down_second,
    up_tiles, down_tiles, up_rows, down_rows, up_out, down_out, in_sems, out_sems,
):
    early = up_first.shape[0]
    late = up_second.shape[0]
    groups = early + late
    slices = volume_ref.shape[1]
    band_rows = volume_ref.shape[2]
    tiles = up_first.shape[3] // 128

    def fetch(index, side, count, act):
        buffer = (up_tiles, down_tiles)[side]
        first = 0 if side == 0 else band_rows - count
        place = 0 if side == 0 else 16 - count
        copy = pltpu.make_async_copy(
            volume_ref.at[:, index, pl.ds(first, count), :],
            buffer.at[index, :, pl.ds(place, count), :],
            in_sems.at[side, index],
        )
        act(copy)

    def each_size(needed, act):
        @pl.when((needed > 0) & (needed <= 8))
        def _():
            act(8)

        @pl.when(needed > 8)
        def _():
            act(16)

    def start_slice(index, carry):
        shift = shear_rows[index]
        each_size(rows_from_high(shift), lambda n: fetch(index, 0, n, lambda c: c.start()))
        each_size(rows_from_low(shift), lambda n: fetch(index, 1, n, lambda c: c.start()))
        return carry

    lax.fori_loop(0, slices, start_slice, 0)

    def scatter(index, side, count, row):
        fetch(index, side, count, lambda c: c.wait())
        source = (up_tiles, down_tiles)[side]
        target = (up_rows, down_rows)[side]
        first = 0 if side == 0 else 16 - count

        def body(tile, carry):
            lane = pl.multiple_of(tile * 128, 128)
            for channel in range(4):
                target[tile, channel, pl.ds(row, count), :] = source[
                    index, channel, first : first + count, pl.ds(lane, 128)
                ].astype(jnp.float32)
            return carry

        lax.fori_loop(0, tiles, body, 0, unroll=PACK_UNROLL)

    def pack_slice(index, used):
        up_used, down_used = used
        shift = shear_rows[index]
        up_count = rows_from_high(shift)
        down_count = rows_from_low(shift)
        down_stop = groups * 8 + 16 - down_used
        each_size(up_count, lambda n: scatter(index, 0, n, up_used))
        each_size(down_count, lambda n: scatter(index, 1, n, down_stop - n))
        return up_used + up_count, down_used + down_count

    lax.fori_loop(0, slices, pack_slice, (0, 0))

    def flush(group, side):
        source = (up_rows, down_rows)[side]
        target = (up_out, down_out)[side]

        def body(tile, carry):
            lanes = pl.ds(pl.multiple_of(tile * 128, 128), 128)
            row = pl.multiple_of(group * 8 + 16 * side, 8)
            for channel in range(4):
                target[group, channel, :, lanes] = source[tile, channel, pl.ds(row, 8), :].astype(
                    jnp.bfloat16
                )
            return carry

        lax.fori_loop(0, tiles, body, 0, unroll=PACK_UNROLL)

    chunks = (
        (up_first, 0, 0, early),
        (down_first, 1, late, early),
        (up_second, 0, early, late),
        (down_second, 1, 0, late),
    )

    def send(target, side, group, first):
        source = (up_out, down_out)[side]
        return pltpu.make_async_copy(
            source.at[group], target.at[group - first], out_sems.at[side, group]
        )

    for target, side, first, count in chunks:

        def start(group, carry):
            flush(group, side)
            send(target, side, group, first).start()
            return carry

        lax.fori_loop(first, first + count, start, 0)
    for target, side, first, count in chunks:

        def finish(group, carry):
            send(target, side, group, first).wait()
            return carry

        lax.fori_loop(first, first + count, finish, 0)


def pack_halo(volume, shear_rows, early, late):
    _, slices, _, columns = volume.shape
    groups = early + late

    def packed(count):
        return jax.ShapeDtypeStruct((count, 4, 8, columns), jnp.bfloat16)

    tiles = pltpu.VMEM((slices, 4, 16, columns), jnp.bfloat16)
    rows = pltpu.VMEM((columns // 128, 4, groups * 8 + 16, 128), jnp.float32)
    out = pltpu.VMEM((groups, 4, 8, columns), jnp.bfloat16)
    return pl.pallas_call(
        pack_kernel,
        out_shape=(packed(early), packed(late), packed(early), packed(late)),
        grid_spec=pltpu.PrefetchScalarGridSpec(
            num_scalar_prefetch=1,
            grid=(1,),
            in_specs=[pl.BlockSpec(memory_space=pl.ANY)],
            out_specs=[pl.BlockSpec(memory_space=pl.ANY)] * 4,
            scratch_shapes=[
                tiles, tiles, rows, rows, out, out,
                pltpu.SemaphoreType.DMA((2, slices)),
                pltpu.SemaphoreType.DMA((2, groups)),
            ],
        ),
        compiler_params=pltpu.CompilerParams(vmem_limit_bytes=VMEM_LIMIT),
    )(shear_rows, volume)


def shear_kernel(part, *refs):
    shear_rows, shear_cols, bounds, volume_ref = refs[:4]
    if part == "front":
        low_refs, high_refs = [refs[4]], [refs[5]]
        before_ref, total, premult, bands, weights, halo, slabs, sems, slab_sems = None, *refs[6:]
    else:
        low_refs, high_refs = [refs[5], refs[4]], [refs[6], refs[7]]
        before_ref, image_ref, premult, bands, weights, halo, slabs, sems, slab_sems, total = refs[8:]
    begin = bounds[0]
    end = bounds[1]
    band_rows = volume_ref.shape[2]
    columns = volume_ref.shape[3]
    blocks = columns // BLOCK
    groups = halo.shape[1]
    stacked = min(GROUP, blocks)

    def fetch(index):
        slot = lax.rem(index, DEPTH)
        return pltpu.make_async_copy(volume_ref.at[:, index], slabs.at[slot], slab_sems.at[slot])

    copies = []
    for side, packed in enumerate((low_refs, high_refs)):
        first = 0
        for ref in packed:
            count = ref.shape[0]
            copies.append((ref, halo.at[side, pl.ds(first, count)]))
            first += count
    if before_ref is not None:
        copies.append((before_ref, total))
    copies = [
        pltpu.make_async_copy(source, target, sems.at[place])
        for place, (source, target) in enumerate(copies)
    ]

    for ahead in range(DEPTH - 1):

        @pl.when(begin + ahead < end)
        def _():
            fetch(begin + ahead).start()

    for copy in copies:
        copy.start()
    none = jnp.zeros((bands.shape[1], EDGE), jnp.bfloat16)
    bands[0, :, 0:EDGE] = none
    bands[blocks, :, EDGE:] = none
    if before_ref is None:

        def clear(block, carry):
            start = pl.multiple_of(block * BLOCK, BLOCK)
            for channel in range(4):
                total[channel, :, pl.ds(start, BLOCK)] = jnp.full(
                    (band_rows, BLOCK), 0.0 if channel < 3 else 1.0, jnp.float32
                )
            return carry

        lax.fori_loop(0, blocks, clear, 0)

    def add(earlier, carry):
        shift = shear_rows[earlier]
        return carry[0] + rows_from_low(shift), carry[1] + rows_from_high(shift)

    def shear_slice(index, slot, used):
        row_shift = shear_rows[index]
        col_shift = shear_cols[index]
        low_count = rows_from_low(row_shift)
        high_count = rows_from_high(row_shift)
        low_start = groups * 8 - used[0] - low_count
        high_start = used[1]

        def premultiply(load, row, count):
            def body(block, carry):
                start = pl.multiple_of(block * BLOCK, BLOCK)
                opacity = load(3, start)
                for channel in range(4):
                    value = opacity
                    if channel < 3:
                        value = load(channel, start) * opacity
                    for half in range(BLOCK // 128):
                        premult[
                            block * (BLOCK // 128) + half, channel, pl.ds(row, count), :
                        ] = value[:, half * 128 : half * 128 + 128]
                return carry

            lax.fori_loop(0, columns // BLOCK, body, 0, unroll=PREMULT_UNROLL)

        @pl.when(index == begin)
        def _():
            for copy in copies:
                copy.wait()

        def rim_of(side, carry):
            packed_row = jnp.where(side == 0, low_start, high_start)
            group = jnp.minimum(packed_row // 8, groups - 2)
            place = jnp.where(side == 0, 16 - low_count, 16 + band_rows)
            for half in range(2):
                premultiply(
                    lambda channel, start: halo[
                        side, group + half, channel, :, pl.ds(start, BLOCK)
                    ].astype(jnp.float32),
                    place - (packed_row - group * 8) + 8 * half,
                    8,
                )
            return carry

        lax.fori_loop(
            jnp.where(low_count > 0, 0, 1), jnp.where(high_count > 0, 2, 1), rim_of, 0
        )
        premultiply(
            lambda channel, start: slabs[slot, channel, :, pl.ds(start, BLOCK)].astype(
                jnp.float32
            ),
            16,
            band_rows,
        )

        source = lax.broadcasted_iota(jnp.int32, (2 * BLOCK, BLOCK), 0)
        target = lax.broadcasted_iota(jnp.int32, (2 * BLOCK, BLOCK), 1)
        distance = jnp.abs(source - target - EDGE - col_shift)
        weights[...] = jnp.where(
            distance == 0, 0.125, jnp.where(distance == 1, 0.0625, 0.0)
        ).astype(jnp.bfloat16)

        def filter_rows(block, half, tile):
            for channel in range(4):
                first, middle, last = (
                    premult[tile, channel, pl.ds(16 + row_shift + shift, band_rows), :]
                    for shift in (-1, 0, 1)
                )
                bands[
                    block,
                    channel * band_rows : (channel + 1) * band_rows,
                    half * 128 : half * 128 + 128,
                ] = (first + last + (middle + middle)).astype(jnp.bfloat16)

        def filter_block(block, carry):
            for half in range(2):
                filter_rows(block, half, block * 2 - 1 + half)
            return carry

        filter_rows(0, 1, 0)
        filter_rows(blocks, 0, columns // 128 - 1)
        lax.fori_loop(1, blocks, filter_block, 0, unroll=ROW_UNROLL)

        def composite(step, carry):
            first = step * stacked
            here = bands[pl.ds(first, stacked)].reshape(stacked * 4 * band_rows, BLOCK)
            after = bands[pl.ds(first + 1, stacked)].reshape(stacked * 4 * band_rows, BLOCK)
            sheared = jnp.dot(
                here, weights[0:BLOCK, :], preferred_element_type=jnp.float32
            ) + jnp.dot(after, weights[BLOCK:, :], preferred_element_type=jnp.float32)
            for block in range(stacked):
                lanes = pl.ds(pl.multiple_of((first + block) * BLOCK, BLOCK), BLOCK)
                top = block * 4 * band_rows
                parts = [
                    sheared[top + channel * band_rows : top + (channel + 1) * band_rows]
                    for channel in range(4)
                ]
                passed = total[3, :, lanes]
                for channel in range(3):
                    total[channel, :, lanes] = total[channel, :, lanes] + passed * parts[channel]
                total[3, :, lanes] = passed - passed * parts[3]
            return carry

        lax.fori_loop(0, blocks // stacked, composite, 0)

    def one_slice(index, used):
        fetch(index).wait()

        @pl.when(index + DEPTH - 1 < end)
        def _():
            fetch(index + DEPTH - 1).start()

        shear_slice(index, lax.rem(index, DEPTH), used)
        return add(index, used)

    lax.fori_loop(begin, end, one_slice, lax.fori_loop(0, begin, add, (0, 0)))
    if part == "back":
        emit_tiles(total, image_ref)


def emit_tiles(total, image_ref):
    _, band_rows, columns = total.shape
    tiles = image_ref.shape[0]
    width = columns // tiles
    lane = lax.broadcasted_iota(jnp.int32, (band_rows, EDGE), 1)

    def value(channel, start, size):
        part = total[channel, :, pl.ds(pl.multiple_of(start, EDGE), size)]
        return part if channel < 3 else 1.0 - part

    def body(tile, carry):
        first = tile * width
        for channel in range(4):
            image_ref[tile, channel, :, 0:width] = value(channel, first, width).astype(
                jnp.bfloat16
            )
            before = value(channel, jnp.maximum(first - EDGE, 0), EDGE)
            after = value(channel, jnp.minimum(first + width, columns - EDGE), EDGE)
            before = jnp.where(tile > 0, before, 0.0)
            after = jnp.where(tile < tiles - 1, after, 0.0)
            image_ref[tile, channel, :, width:] = jnp.where(
                lane < EDGE // 2, after, before
            ).astype(jnp.bfloat16)
        return carry

    lax.fori_loop(0, tiles, body, 0)


def shear_part(part, bounds, volume, shear_rows, shear_cols, packed, before, tiles):
    _, _, band_rows, columns = volume.shape
    groups = sum(chunk.shape[0] for chunk in packed) // 2

    outside = list(packed) + ([] if before is None else [before])
    total_shape = (4, band_rows, columns)
    scratch = [
        pltpu.VMEM((columns // 128, 4, band_rows + 32, 128), jnp.float32),
        pltpu.VMEM((columns // BLOCK + 1, 4 * band_rows, BLOCK), jnp.bfloat16),
        pltpu.VMEM((2 * BLOCK, BLOCK), jnp.bfloat16),
        pltpu.VMEM((2, groups, 4, 8, columns), jnp.bfloat16),
        pltpu.VMEM((DEPTH, 4, band_rows, columns), jnp.bfloat16),
        pltpu.SemaphoreType.DMA((len(outside),)),
        pltpu.SemaphoreType.DMA((DEPTH,)),
    ]
    if part == "front":
        out = jax.ShapeDtypeStruct(total_shape, jnp.float32)
    else:
        image = (tiles, 4, band_rows, columns // tiles + EDGE)
        out = jax.ShapeDtypeStruct(image, jnp.bfloat16)
        scratch.append(pltpu.VMEM(total_shape, jnp.float32))
    whole = len(out.shape)
    return pl.pallas_call(
        functools.partial(shear_kernel, part),
        out_shape=out,
        grid_spec=pltpu.PrefetchScalarGridSpec(
            num_scalar_prefetch=3,
            grid=(1,),
            in_specs=[pl.BlockSpec(memory_space=pl.ANY)] * (1 + len(outside)),
            out_specs=pl.BlockSpec(
                out.shape, lambda i, a, b, c: (0,) * whole, pipeline_mode=pl.Buffered(1)
            ),
            scratch_shapes=scratch,
        ),
        compiler_params=pltpu.CompilerParams(vmem_limit_bytes=VMEM_LIMIT),
        cost_estimate=pl.CostEstimate(
            flops=2 * 512 * volume.size, transcendentals=0, bytes_accessed=volume.size
        ),
    )(shear_rows, shear_cols, bounds, volume, *outside)


def weight_of(offset):
    return jnp.where(offset == 0, 0.5, jnp.where(jnp.abs(offset) == 1, 0.25, 0.0))


def across_kernel(pieces_ref, shifts_ref, across_ref, top_ref, bottom_ref):
    tiles, _, band_rows, padded = pieces_ref.shape
    width = across_ref.shape[2]
    for row in range(0, band_rows, 8):
        rows = slice(row, row + 8)
        totals = [None] * 4
        passed = None
        for tile in range(tiles):
            parts = [pieces_ref[tile, channel, rows, :].astype(jnp.float32) for channel in range(4)]
            if tile == 0:
                totals = parts[:3]
                passed = 1.0 - parts[3]
            else:
                totals = [total + passed * part for total, part in zip(totals, parts[:3])]
                passed = passed - passed * parts[3]
        totals = totals[:3] + [1.0 - passed]
        shifts = jnp.broadcast_to(shifts_ref[rows, :], (8, width))
        results = [jnp.zeros((8, width), jnp.float32)] * 4
        for offset in range(-RIM, RIM + 1):
            factor = weight_of(offset - shifts)
            for channel in range(4):
                moved = pltpu.roll(totals[channel], (-offset) % padded, 1)[:, :width]
                results[channel] = results[channel] + factor * moved
        for channel in range(4):
            across_ref[channel, rows, :] = results[channel]
    for channel in range(4):
        top_ref[channel * RIM : (channel + 1) * RIM, :] = across_ref[channel, 0:RIM, :]
        bottom_ref[channel * RIM : (channel + 1) * RIM, :] = across_ref[
            channel, band_rows - RIM : band_rows, :
        ]


def warp_columns(pieces, shifts, width):
    _, _, band_rows, _ = pieces.shape
    rim = jax.ShapeDtypeStruct((4 * RIM, width), jnp.float32)
    return pl.pallas_call(
        across_kernel,
        out_shape=(jax.ShapeDtypeStruct((4, band_rows, width), jnp.float32), rim, rim),
        compiler_params=pltpu.CompilerParams(vmem_limit_bytes=VMEM_LIMIT),
    )(pieces, shifts)


def final_kernel(across_ref, low_ref, high_ref, shifts_ref, final_ref, extended):
    _, band_rows, width = across_ref.shape
    for channel in range(4):
        extended[channel, 16 : 16 + band_rows, :] = across_ref[channel]
        rim = slice(channel * RIM, (channel + 1) * RIM)
        extended[channel, 16 - RIM : 16, :] = low_ref[rim, :]
        extended[channel, 16 + band_rows : 16 + band_rows + RIM, :] = high_ref[rim, :]
    for lane in range(0, width, 128):
        lanes = slice(lane, lane + 128)
        shifts = jnp.broadcast_to(shifts_ref[:, lanes], (8, 128))
        factors = [weight_of(offset - shifts) for offset in range(-RIM, RIM + 1)]
        for channel in range(4):
            for row in range(0, band_rows, 8):
                result = jnp.zeros((8, 128), jnp.float32)
                for offset in range(-RIM, RIM + 1):
                    start = 16 + row + offset
                    result = result + factors[offset + RIM] * extended[
                        channel, start : start + 8, lanes
                    ]
                final_ref[channel, row : row + 8, lanes] = result


def warp_rows_of(across, low, high, shifts):
    _, band_rows, width = across.shape
    return pl.pallas_call(
        final_kernel,
        out_shape=jax.ShapeDtypeStruct(across.shape, jnp.float32),
        scratch_shapes=[pltpu.VMEM((4, band_rows + 32, width), jnp.float32)],
        compiler_params=pltpu.CompilerParams(vmem_limit_bytes=VMEM_LIMIT),
    )(across, low, high, shifts)


def neighbours(axis):
    count = lax.axis_size(axis)
    forward = [(i, i + 1) for i in range(count - 1)]
    return forward, [(target, source) for source, target in forward]


def per_device(volume, shear_rows, shear_cols, warp_cols, warp_rows):
    band_rows = volume.shape[2]
    columns = volume.shape[3]
    tiles = lax.axis_size("depth")
    width = columns // tiles
    forward, backward = neighbours("rows")
    slices = volume.shape[1]
    most = -(-RIM * slices // 8)
    sizes = [size for size in SIZES if size < most] + [most]
    earlier = jnp.arange(slices)[None, :] <= jnp.arange(slices)[:, None]
    reach = jnp.maximum(
        jnp.sum(jnp.where(earlier, rows_from_high(shear_rows)[None, :], 0), 1),
        jnp.sum(jnp.where(earlier, rows_from_low(shear_rows)[None, :], 0), 1),
    )
    needed = reach[slices - 1]
    choice = sum((needed > 8 * size).astype(jnp.int32) for size in sizes[:-1])

    def with_groups(groups):
        early = (groups + 1) // 2
        late = groups - early

        def branch(volume, shear_rows, shear_cols, reach):
            middle = jnp.minimum(jnp.sum((reach <= 8 * early).astype(jnp.int32)), slices - 1)
            begin, end = jnp.zeros_like(middle), jnp.full_like(middle, slices)
            up_first, up_second, down_first, down_second = pack_halo(
                volume, shear_rows, early, late
            )
            high_first = lax.ppermute(up_first, "rows", backward)
            low_first = lax.ppermute(down_first, "rows", forward)
            if ORDERED:
                high_first, low_first, up_second, down_second = lax.optimization_barrier(
                    (high_first, low_first, up_second, down_second)
                )
            high_second = lax.ppermute(up_second, "rows", backward)
            low_second = lax.ppermute(down_second, "rows", forward)
            total = shear_part(
                "front", jnp.stack([begin, middle]), volume, shear_rows, shear_cols,
                (low_first, high_first), None, tiles,
            )
            return shear_part(
                "back", jnp.stack([middle, end]), volume, shear_rows, shear_cols,
                (low_first, low_second, high_first, high_second), total, tiles,
            )

        return branch

    image = lax.switch(
        choice, [with_groups(groups) for groups in sizes], volume, shear_rows, shear_cols, reach
    )
    pieces = lax.all_to_all(image, "depth", 0, 0, tiled=True)
    row_start = lax.axis_index("rows") * band_rows
    row_shifts = lax.dynamic_slice_in_dim(warp_cols, row_start, band_rows, 0)
    across, top, bottom = warp_columns(pieces, row_shifts[:, None], width)
    below = lax.ppermute(bottom, "rows", forward)
    above = lax.ppermute(top, "rows", backward)
    return warp_rows_of(across, below, above, warp_rows[None, :])


def solution(mesh):
    return jax.shard_map(
        per_device,
        mesh=mesh,
        in_specs=(P(None, "depth", "rows", None), P("depth"), P("depth"), P(), P("depth")),
        out_specs=P(None, "rows", "depth"),
        check_vma=False,
    )
```

```python
import functools

import jax
import jax.numpy as jnp
from jax import lax
from jax.experimental import pallas as pl
from jax.experimental.pallas import tpu as pltpu
from jax.sharding import PartitionSpec as P

SHIFT = 8
RIM = SHIFT + 1
BLOCK = 256
GROUP = 16
ROW_UNROLL = 3
PREMULT_UNROLL = 2
PACK_UNROLL = 8
DEPTH = 4
SIZES = (6, 7, 8, 9, 10, 12)
EDGE = 128
VMEM_LIMIT = 60 * 1024 * 1024


def rows_from_high(shift):
    return jnp.maximum(shift + 1, 0)


def rows_from_low(shift):
    return jnp.maximum(1 - shift, 0)


def pack_kernel(
    first_row, shear_rows, volume_ref, up_ref, down_ref,
    up_tiles, down_tiles, up_rows, down_rows, up_out, down_out, in_sems, out_sems,
):
    groups = up_ref.shape[0]
    slices = volume_ref.shape[1]
    band_rows = volume_ref.shape[2]
    tiles = up_ref.shape[3] // 128
    chunk_rows = groups * 8
    row_bufs = (up_rows, down_rows)

    def fetch(index, side, count):
        buffer = (up_tiles, down_tiles)[side]
        first = 0 if side == 0 else band_rows - count
        place = 0 if side == 0 else 16 - count
        return pltpu.make_async_copy(
            volume_ref.at[:, index, pl.ds(first, count), :],
            buffer.at[index, :, pl.ds(place, count), :],
            in_sems.at[side, index],
        )

    def each_size(needed, used, act):
        in_chunk = (used < first_row + chunk_rows) & (used + needed > first_row)

        @pl.when(in_chunk & (needed > 0) & (needed <= 8))
        def _():
            act(8)

        @pl.when(in_chunk & (needed > 8))
        def _():
            act(16)

    def scatter(index, side, count, row):
        fetch(index, side, count).wait()
        source = (up_tiles, down_tiles)[side]
        target = row_bufs[side]
        first = 0 if side == 0 else 16 - count

        def body(tile, carry):
            lane = pl.multiple_of(tile * 128, 128)
            for channel in range(4):
                target[tile, channel, pl.ds(row, count), :] = source[
                    index, channel, first : first + count, pl.ds(lane, 128)
                ].astype(jnp.float32)
            return carry

        lax.fori_loop(0, tiles, body, 0, unroll=PACK_UNROLL)

    def for_slices(act):
        def body(index, used):
            shift = shear_rows[index]
            counts = rows_from_high(shift), rows_from_low(shift)
            for side in range(2):
                each_size(counts[side], used[side], functools.partial(act, index, side, used[side]))
            return used[0] + counts[0], used[1] + counts[1]

        lax.fori_loop(0, slices, body, (0, 0))

    def start(index, side, used, count):
        fetch(index, side, count).start()

    def place(index, side, used, count):
        row = used - first_row + 16
        scatter(index, side, count, row if side == 0 else chunk_rows + 32 - row - count)

    for_slices(start)
    for_slices(place)

    def send(side, group):
        return pltpu.make_async_copy(
            (up_out, down_out)[side].at[group], (up_ref, down_ref)[side].at[group], out_sems.at[side, group]
        )

    def flush(group, carry):
        row = pl.multiple_of(group * 8 + 16, 8)
        for side, target in enumerate((up_out, down_out)):

            def body(tile, carry):
                lanes = pl.ds(pl.multiple_of(tile * 128, 128), 128)
                for channel in range(4):
                    target[group, channel, :, lanes] = row_bufs[side][
                        tile, channel, pl.ds(row, 8), :
                    ].astype(jnp.bfloat16)
                return carry

            lax.fori_loop(0, tiles, body, 0, unroll=PACK_UNROLL)
            send(side, group).start()
        return carry

    def finish(group, carry):
        for side in range(2):
            send(side, group).wait()
        return carry

    lax.fori_loop(0, groups, flush, 0)
    lax.fori_loop(0, groups, finish, 0)


def pack_halo(volume, shear_rows, first, groups):
    _, slices, _, columns = volume.shape
    packed = jax.ShapeDtypeStruct((groups, 4, 8, columns), jnp.bfloat16)
    tiles = pltpu.VMEM((slices, 4, 16, columns), jnp.bfloat16)
    rows = pltpu.VMEM((columns // 128, 4, groups * 8 + 32, 128), jnp.float32)
    out = pltpu.VMEM((groups, 4, 8, columns), jnp.bfloat16)
    return pl.pallas_call(
        functools.partial(pack_kernel, first * 8),
        out_shape=(packed, packed),
        grid_spec=pltpu.PrefetchScalarGridSpec(
            num_scalar_prefetch=1,
            grid=(1,),
            in_specs=[pl.BlockSpec(memory_space=pl.ANY)],
            out_specs=[pl.BlockSpec(memory_space=pl.ANY)] * 2,
            scratch_shapes=[
                tiles, tiles, rows, rows, out, out,
                pltpu.SemaphoreType.DMA((2, slices)),
                pltpu.SemaphoreType.DMA((2, groups)),
            ],
        ),
        compiler_params=pltpu.CompilerParams(vmem_limit_bytes=VMEM_LIMIT),
        cost_estimate=pl.CostEstimate(
            flops=volume.size // 16, transcendentals=0, bytes_accessed=volume.size // 4
        ),
    )(shear_rows, volume)


def shear_kernel(part, *refs):
    shear_rows, shear_cols, bounds, volume_ref = refs[:4]
    if part == "front":
        low_refs, high_refs = [refs[4]], [refs[5]]
        before_ref, total, premult, bands, weights, halo, slabs, sems, slab_sems = None, *refs[6:]
    else:
        low_refs, high_refs = [refs[5], refs[4]], [refs[6], refs[7]]
        before_ref, image_ref, premult, bands, weights, halo, slabs, sems, slab_sems, total = refs[8:]
    begin = bounds[0]
    end = bounds[1]
    band_rows = volume_ref.shape[2]
    columns = volume_ref.shape[3]
    blocks = columns // BLOCK
    groups = halo.shape[1]
    stacked = min(GROUP, blocks)

    def fetch(index):
        slot = lax.rem(index, DEPTH)
        return pltpu.make_async_copy(volume_ref.at[:, index], slabs.at[slot], slab_sems.at[slot])

    copies = []
    for side, packed in enumerate((low_refs, high_refs)):
        first = 0
        for ref in packed:
            count = ref.shape[0]
            copies.append((ref, halo.at[side, pl.ds(first, count)]))
            first += count
    if before_ref is not None:
        copies.append((before_ref, total))
    copies = [
        pltpu.make_async_copy(source, target, sems.at[place])
        for place, (source, target) in enumerate(copies)
    ]

    for ahead in range(DEPTH - 1):

        @pl.when(begin + ahead < end)
        def _():
            fetch(begin + ahead).start()

    for copy in copies:
        copy.start()
    none = jnp.zeros((bands.shape[1], EDGE), jnp.bfloat16)
    bands[0, :, 0:EDGE] = none
    bands[blocks, :, EDGE:] = none
    if before_ref is None:

        def clear(block, carry):
            start = pl.multiple_of(block * BLOCK, BLOCK)
            for channel in range(4):
                total[channel, :, pl.ds(start, BLOCK)] = jnp.full(
                    (band_rows, BLOCK), 0.0 if channel < 3 else 1.0, jnp.float32
                )
            return carry

        lax.fori_loop(0, blocks, clear, 0)

    def add(earlier, carry):
        shift = shear_rows[earlier]
        return carry[0] + rows_from_low(shift), carry[1] + rows_from_high(shift)

    def shear_slice(index, slot, used):
        row_shift = shear_rows[index]
        col_shift = shear_cols[index]
        low_count = rows_from_low(row_shift)
        high_count = rows_from_high(row_shift)
        low_start = groups * 8 - used[0] - low_count
        high_start = used[1]

        def premultiply(load, row, count):
            def body(block, carry):
                start = pl.multiple_of(block * BLOCK, BLOCK)
                opacity = load(3, start)
                for channel in range(4):
                    value = opacity
                    if channel < 3:
                        value = load(channel, start) * opacity
                    for half in range(BLOCK // 128):
                        premult[
                            block * (BLOCK // 128) + half, channel, pl.ds(row, count), :
                        ] = value[:, half * 128 : half * 128 + 128]
                return carry

            lax.fori_loop(0, columns // BLOCK, body, 0, unroll=PREMULT_UNROLL)

        @pl.when(index == begin)
        def _():
            for copy in copies:
                copy.wait()

        def rim_of(side, carry):
            packed_row = jnp.where(side == 0, low_start, high_start)
            group = jnp.minimum(packed_row // 8, groups - 2)
            place = jnp.where(side == 0, 16 - low_count, 16 + band_rows)
            for half in range(2):
                premultiply(
                    lambda channel, start: halo[
                        side, group + half, channel, :, pl.ds(start, BLOCK)
                    ].astype(jnp.float32),
                    place - (packed_row - group * 8) + 8 * half,
                    8,
                )
            return carry

        lax.fori_loop(
            jnp.where(low_count > 0, 0, 1), jnp.where(high_count > 0, 2, 1), rim_of, 0
        )
        premultiply(
            lambda channel, start: slabs[slot, channel, :, pl.ds(start, BLOCK)].astype(
                jnp.float32
            ),
            16,
            band_rows,
        )

        source = lax.broadcasted_iota(jnp.int32, (2 * BLOCK, BLOCK), 0)
        target = lax.broadcasted_iota(jnp.int32, (2 * BLOCK, BLOCK), 1)
        distance = jnp.abs(source - target - EDGE - col_shift)
        weights[...] = jnp.where(
            distance == 0, 0.125, jnp.where(distance == 1, 0.0625, 0.0)
        ).astype(jnp.bfloat16)

        def filter_rows(block, half, tile):
            for channel in range(4):
                first, middle, last = (
                    premult[tile, channel, pl.ds(16 + row_shift + shift, band_rows), :]
                    for shift in (-1, 0, 1)
                )
                bands[
                    block,
                    channel * band_rows : (channel + 1) * band_rows,
                    half * 128 : half * 128 + 128,
                ] = (first + last + (middle + middle)).astype(jnp.bfloat16)

        def filter_block(block, carry):
            for half in range(2):
                filter_rows(block, half, block * 2 - 1 + half)
            return carry

        filter_rows(0, 1, 0)
        filter_rows(blocks, 0, columns // 128 - 1)
        lax.fori_loop(1, blocks, filter_block, 0, unroll=ROW_UNROLL)

        def composite(step, carry):
            first = step * stacked
            here = bands[pl.ds(first, stacked)].reshape(stacked * 4 * band_rows, BLOCK)
            after = bands[pl.ds(first + 1, stacked)].reshape(stacked * 4 * band_rows, BLOCK)
            sheared = jnp.dot(
                here, weights[0:BLOCK, :], preferred_element_type=jnp.float32
            ) + jnp.dot(after, weights[BLOCK:, :], preferred_element_type=jnp.float32)
            for block in range(stacked):
                lanes = pl.ds(pl.multiple_of((first + block) * BLOCK, BLOCK), BLOCK)
                top = block * 4 * band_rows
                parts = [
                    sheared[top + channel * band_rows : top + (channel + 1) * band_rows]
                    for channel in range(4)
                ]
                passed = total[3, :, lanes]
                for channel in range(3):
                    total[channel, :, lanes] = total[channel, :, lanes] + passed * parts[channel]
                total[3, :, lanes] = passed - passed * parts[3]
            return carry

        lax.fori_loop(0, blocks // stacked, composite, 0)

    def one_slice(index, used):
        fetch(index).wait()

        @pl.when(index + DEPTH - 1 < end)
        def _():
            fetch(index + DEPTH - 1).start()

        shear_slice(index, lax.rem(index, DEPTH), used)
        return add(index, used)

    lax.fori_loop(begin, end, one_slice, lax.fori_loop(0, begin, add, (0, 0)))
    if part == "back":
        emit_tiles(total, image_ref)


def emit_tiles(total, image_ref):
    _, band_rows, columns = total.shape
    tiles = image_ref.shape[0]
    width = columns // tiles
    lane = lax.broadcasted_iota(jnp.int32, (band_rows, EDGE), 1)

    def value(channel, start, size):
        part = total[channel, :, pl.ds(pl.multiple_of(start, EDGE), size)]
        return part if channel < 3 else 1.0 - part

    def body(tile, carry):
        first = tile * width
        for channel in range(4):
            image_ref[tile, channel, :, 0:width] = value(channel, first, width).astype(
                jnp.bfloat16
            )
            before = value(channel, jnp.maximum(first - EDGE, 0), EDGE)
            after = value(channel, jnp.minimum(first + width, columns - EDGE), EDGE)
            before = jnp.where(tile > 0, before, 0.0)
            after = jnp.where(tile < tiles - 1, after, 0.0)
            image_ref[tile, channel, :, width:] = jnp.where(
                lane < EDGE // 2, after, before
            ).astype(jnp.bfloat16)
        return carry

    lax.fori_loop(0, tiles, body, 0)


def shear_part(part, bounds, volume, shear_rows, shear_cols, packed, before, tiles):
    _, _, band_rows, columns = volume.shape
    groups = sum(chunk.shape[0] for chunk in packed) // 2

    outside = list(packed) + ([] if before is None else [before])
    total_shape = (4, band_rows, columns)
    scratch = [
        pltpu.VMEM((columns // 128, 4, band_rows + 32, 128), jnp.float32),
        pltpu.VMEM((columns // BLOCK + 1, 4 * band_rows, BLOCK), jnp.bfloat16),
        pltpu.VMEM((2 * BLOCK, BLOCK), jnp.bfloat16),
        pltpu.VMEM((2, groups, 4, 8, columns), jnp.bfloat16),
        pltpu.VMEM((DEPTH, 4, band_rows, columns), jnp.bfloat16),
        pltpu.SemaphoreType.DMA((len(outside),)),
        pltpu.SemaphoreType.DMA((DEPTH,)),
    ]
    if part == "front":
        out = jax.ShapeDtypeStruct(total_shape, jnp.float32)
    else:
        image = (tiles, 4, band_rows, columns // tiles + EDGE)
        out = jax.ShapeDtypeStruct(image, jnp.bfloat16)
        scratch.append(pltpu.VMEM(total_shape, jnp.float32))
    whole = len(out.shape)
    return pl.pallas_call(
        functools.partial(shear_kernel, part),
        out_shape=out,
        grid_spec=pltpu.PrefetchScalarGridSpec(
            num_scalar_prefetch=3,
            grid=(1,),
            in_specs=[pl.BlockSpec(memory_space=pl.ANY)] * (1 + len(outside)),
            out_specs=pl.BlockSpec(
                out.shape, lambda i, a, b, c: (0,) * whole, pipeline_mode=pl.Buffered(1)
            ),
            scratch_shapes=scratch,
        ),
        compiler_params=pltpu.CompilerParams(vmem_limit_bytes=VMEM_LIMIT),
        cost_estimate=pl.CostEstimate(
            flops=2 * 512 * volume.size, transcendentals=0, bytes_accessed=volume.size
        ),
    )(shear_rows, shear_cols, bounds, volume, *outside)


def weight_of(offset):
    return jnp.where(offset == 0, 0.5, jnp.where(jnp.abs(offset) == 1, 0.25, 0.0))


def across_kernel(pieces_ref, shifts_ref, across_ref, top_ref, bottom_ref):
    tiles, _, band_rows, padded = pieces_ref.shape
    width = across_ref.shape[2]
    for row in range(0, band_rows, 8):
        rows = slice(row, row + 8)
        totals = [None] * 4
        passed = None
        for tile in range(tiles):
            parts = [pieces_ref[tile, channel, rows, :].astype(jnp.float32) for channel in range(4)]
            if tile == 0:
                totals = parts[:3]
                passed = 1.0 - parts[3]
            else:
                totals = [total + passed * part for total, part in zip(totals, parts[:3])]
                passed = passed - passed * parts[3]
        totals = totals[:3] + [1.0 - passed]
        shifts = jnp.broadcast_to(shifts_ref[rows, :], (8, width))
        results = [jnp.zeros((8, width), jnp.float32)] * 4
        for offset in range(-RIM, RIM + 1):
            factor = weight_of(offset - shifts)
            for channel in range(4):
                moved = pltpu.roll(totals[channel], (-offset) % padded, 1)[:, :width]
                results[channel] = results[channel] + factor * moved
        for channel in range(4):
            across_ref[channel, rows, :] = results[channel]
    for channel in range(4):
        top_ref[channel * RIM : (channel + 1) * RIM, :] = across_ref[channel, 0:RIM, :]
        bottom_ref[channel * RIM : (channel + 1) * RIM, :] = across_ref[
            channel, band_rows - RIM : band_rows, :
        ]


def warp_columns(pieces, shifts, width):
    _, _, band_rows, _ = pieces.shape
    rim = jax.ShapeDtypeStruct((4 * RIM, width), jnp.float32)
    return pl.pallas_call(
        across_kernel,
        out_shape=(jax.ShapeDtypeStruct((4, band_rows, width), jnp.float32), rim, rim),
        compiler_params=pltpu.CompilerParams(vmem_limit_bytes=VMEM_LIMIT),
    )(pieces, shifts)


def final_kernel(across_ref, low_ref, high_ref, shifts_ref, final_ref, extended):
    _, band_rows, width = across_ref.shape
    for channel in range(4):
        extended[channel, 16 : 16 + band_rows, :] = across_ref[channel]
        rim = slice(channel * RIM, (channel + 1) * RIM)
        extended[channel, 16 - RIM : 16, :] = low_ref[rim, :]
        extended[channel, 16 + band_rows : 16 + band_rows + RIM, :] = high_ref[rim, :]
    for lane in range(0, width, 128):
        lanes = slice(lane, lane + 128)
        shifts = jnp.broadcast_to(shifts_ref[:, lanes], (8, 128))
        factors = [weight_of(offset - shifts) for offset in range(-RIM, RIM + 1)]
        for channel in range(4):
            for row in range(0, band_rows, 8):
                result = jnp.zeros((8, 128), jnp.float32)
                for offset in range(-RIM, RIM + 1):
                    start = 16 + row + offset
                    result = result + factors[offset + RIM] * extended[
                        channel, start : start + 8, lanes
                    ]
                final_ref[channel, row : row + 8, lanes] = result


def warp_rows_of(across, low, high, shifts):
    _, band_rows, width = across.shape
    return pl.pallas_call(
        final_kernel,
        out_shape=jax.ShapeDtypeStruct(across.shape, jnp.float32),
        scratch_shapes=[pltpu.VMEM((4, band_rows + 32, width), jnp.float32)],
        compiler_params=pltpu.CompilerParams(vmem_limit_bytes=VMEM_LIMIT),
    )(across, low, high, shifts)


def neighbours(axis):
    count = lax.axis_size(axis)
    forward = [(i, i + 1) for i in range(count - 1)]
    return forward, [(target, source) for source, target in forward]


def per_device(volume, shear_rows, shear_cols, warp_cols, warp_rows):
    band_rows = volume.shape[2]
    columns = volume.shape[3]
    tiles = lax.axis_size("depth")
    width = columns // tiles
    forward, backward = neighbours("rows")
    slices = volume.shape[1]
    most = -(-RIM * slices // 8)
    sizes = [size for size in SIZES if size < most] + [most]
    earlier = jnp.arange(slices)[None, :] <= jnp.arange(slices)[:, None]
    reach = jnp.maximum(
        jnp.sum(jnp.where(earlier, rows_from_high(shear_rows)[None, :], 0), 1),
        jnp.sum(jnp.where(earlier, rows_from_low(shear_rows)[None, :], 0), 1),
    )
    needed = reach[slices - 1]
    choice = sum((needed > 8 * size).astype(jnp.int32) for size in sizes[:-1])

    def with_groups(groups):
        early = (groups + 1) // 2
        late = groups - early

        def branch(volume, shear_rows, shear_cols, reach):
            middle = jnp.minimum(jnp.sum((reach <= 8 * early).astype(jnp.int32)), slices - 1)
            begin, end = jnp.zeros_like(middle), jnp.full_like(middle, slices)
            up_first, down_first = pack_halo(volume, shear_rows, 0, early)
            up_second, down_second = pack_halo(volume, shear_rows, early, late)
            high_first = lax.ppermute(up_first, "rows", backward)
            low_first = lax.ppermute(down_first, "rows", forward)
            high_second = lax.ppermute(up_second, "rows", backward)
            low_second = lax.ppermute(down_second, "rows", forward)
            total = shear_part(
                "front", jnp.stack([begin, middle]), volume, shear_rows, shear_cols,
                (low_first, high_first), None, tiles,
            )
            return shear_part(
                "back", jnp.stack([middle, end]), volume, shear_rows, shear_cols,
                (low_first, low_second, high_first, high_second), total, tiles,
            )

        return branch

    image = lax.switch(
        choice, [with_groups(groups) for groups in sizes], volume, shear_rows, shear_cols, reach
    )
    pieces = lax.all_to_all(image, "depth", 0, 0, tiled=True)
    row_start = lax.axis_index("rows") * band_rows
    row_shifts = lax.dynamic_slice_in_dim(warp_cols, row_start, band_rows, 0)
    across, top, bottom = warp_columns(pieces, row_shifts[:, None], width)
    below = lax.ppermute(bottom, "rows", forward)
    above = lax.ppermute(top, "rows", backward)
    return warp_rows_of(across, below, above, warp_rows[None, :])


def solution(mesh):
    return jax.shard_map(
        per_device,
        mesh=mesh,
        in_specs=(P(None, "depth", "rows", None), P("depth"), P("depth"), P(), P("depth")),
        out_specs=P(None, "rows", "depth"),
        check_vma=False,
    )
```

```python
import functools

import jax
import jax.numpy as jnp
from jax import lax
from jax.experimental import pallas as pl
from jax.experimental.pallas import tpu as pltpu
from jax.sharding import PartitionSpec as P

SHIFT = 8
RIM = SHIFT + 1
BLOCK = 256
GROUP = 16
ROW_UNROLL = 3
PREMULT_UNROLL = 2
PACK_UNROLL = 8
DEPTH = 4
SIZES = (6, 7, 8, 9, 10, 12)
EDGE = 128
VMEM_LIMIT = 60 * 1024 * 1024


def rows_from_high(shift):
    return jnp.maximum(shift + 1, 0)


def rows_from_low(shift):
    return jnp.maximum(1 - shift, 0)


def pack_kernel(
    first_row, shear_rows, volume_ref, up_ref, down_ref,
    up_tiles, down_tiles, up_rows, down_rows, up_out, down_out, in_sems, out_sems,
):
    groups = up_ref.shape[0]
    slices = volume_ref.shape[1]
    band_rows = volume_ref.shape[2]
    tiles = up_ref.shape[3] // 128
    chunk_rows = groups * 8
    row_bufs = (up_rows, down_rows)

    def fetch(index, side, count):
        buffer = (up_tiles, down_tiles)[side]
        first = 0 if side == 0 else band_rows - count
        place = 0 if side == 0 else 16 - count
        return pltpu.make_async_copy(
            volume_ref.at[:, index, pl.ds(first, count), :],
            buffer.at[index, :, pl.ds(place, count), :],
            in_sems.at[side, index],
        )

    def each_size(needed, used, act):
        in_chunk = (used < first_row + chunk_rows) & (used + needed > first_row)

        @pl.when(in_chunk & (needed > 0) & (needed <= 8))
        def _():
            act(8)

        @pl.when(in_chunk & (needed > 8))
        def _():
            act(16)

    def scatter(index, side, count, row):
        fetch(index, side, count).wait()
        source = (up_tiles, down_tiles)[side]
        target = row_bufs[side]
        first = 0 if side == 0 else 16 - count

        def body(tile, carry):
            lane = pl.multiple_of(tile * 128, 128)
            for channel in range(4):
                target[tile, channel, pl.ds(row, count), :] = source[
                    index, channel, first : first + count, pl.ds(lane, 128)
                ].astype(jnp.float32)
            return carry

        lax.fori_loop(0, tiles, body, 0, unroll=PACK_UNROLL)

    def for_slices(act):
        def body(index, used):
            shift = shear_rows[index]
            counts = rows_from_high(shift), rows_from_low(shift)
            for side in range(2):
                each_size(counts[side], used[side], functools.partial(act, index, side, used[side]))
            return used[0] + counts[0], used[1] + counts[1]

        lax.fori_loop(0, slices, body, (0, 0))

    def start(index, side, used, count):
        fetch(index, side, count).start()

    def place(index, side, used, count):
        row = used - first_row + 16
        scatter(index, side, count, row if side == 0 else chunk_rows + 32 - row - count)

    for_slices(start)
    for_slices(place)

    def send(side, group):
        return pltpu.make_async_copy(
            (up_out, down_out)[side].at[group], (up_ref, down_ref)[side].at[group], out_sems.at[side, group]
        )

    def flush(group, carry):
        row = pl.multiple_of(group * 8 + 16, 8)
        for side, target in enumerate((up_out, down_out)):

            def body(tile, carry):
                lanes = pl.ds(pl.multiple_of(tile * 128, 128), 128)
                for channel in range(4):
                    target[group, channel, :, lanes] = row_bufs[side][
                        tile, channel, pl.ds(row, 8), :
                    ].astype(jnp.bfloat16)
                return carry

            lax.fori_loop(0, tiles, body, 0, unroll=PACK_UNROLL)
            send(side, group).start()
        return carry

    def finish(group, carry):
        for side in range(2):
            send(side, group).wait()
        return carry

    lax.fori_loop(0, groups, flush, 0)
    lax.fori_loop(0, groups, finish, 0)


def pack_halo(volume, shear_rows, first, groups):
    _, slices, _, columns = volume.shape
    packed = jax.ShapeDtypeStruct((groups, 4, 8, columns), jnp.bfloat16)
    tiles = pltpu.VMEM((slices, 4, 16, columns), jnp.bfloat16)
    rows = pltpu.VMEM((columns // 128, 4, groups * 8 + 32, 128), jnp.float32)
    out = pltpu.VMEM((groups, 4, 8, columns), jnp.bfloat16)
    return pl.pallas_call(
        functools.partial(pack_kernel, first * 8),
        out_shape=(packed, packed),
        grid_spec=pltpu.PrefetchScalarGridSpec(
            num_scalar_prefetch=1,
            grid=(1,),
            in_specs=[pl.BlockSpec(memory_space=pl.ANY)],
            out_specs=[pl.BlockSpec(memory_space=pl.ANY)] * 2,
            scratch_shapes=[
                tiles, tiles, rows, rows, out, out,
                pltpu.SemaphoreType.DMA((2, slices)),
                pltpu.SemaphoreType.DMA((2, groups)),
            ],
        ),
        compiler_params=pltpu.CompilerParams(vmem_limit_bytes=VMEM_LIMIT),
        cost_estimate=pl.CostEstimate(
            flops=volume.size // 16, transcendentals=0, bytes_accessed=volume.size // 4
        ),
    )(shear_rows, volume)


def shear_kernel(part, *refs):
    shear_rows, shear_cols, bounds, volume_ref = refs[:4]
    if part == "front":
        low_refs, high_refs = [refs[4]], [refs[5]]
        before_ref, total, premult, bands, weights, halo, slabs, sems, slab_sems = None, *refs[6:]
    else:
        low_refs, high_refs = [refs[5], refs[4]], [refs[6], refs[7]]
        before_ref, kept_ref, sent_ref, premult, bands, weights, halo, slabs, sems, slab_sems, total = refs[8:]
    begin = bounds[0]
    end = bounds[1]
    band_rows = volume_ref.shape[2]
    columns = volume_ref.shape[3]
    blocks = columns // BLOCK
    groups = halo.shape[1]
    stacked = min(GROUP, blocks)

    def fetch(index):
        slot = lax.rem(index, DEPTH)
        return pltpu.make_async_copy(volume_ref.at[:, index], slabs.at[slot], slab_sems.at[slot])

    copies = []
    for side, packed in enumerate((low_refs, high_refs)):
        first = 0
        for ref in packed:
            count = ref.shape[0]
            copies.append((ref, halo.at[side, pl.ds(first, count)]))
            first += count
    if before_ref is not None:
        copies.append((before_ref, total))
    copies = [
        pltpu.make_async_copy(source, target, sems.at[place])
        for place, (source, target) in enumerate(copies)
    ]

    for ahead in range(DEPTH - 1):

        @pl.when(begin + ahead < end)
        def _():
            fetch(begin + ahead).start()

    for copy in copies:
        copy.start()
    none = jnp.zeros((bands.shape[1], EDGE), jnp.bfloat16)
    bands[0, :, 0:EDGE] = none
    bands[blocks, :, EDGE:] = none
    if before_ref is None:

        def clear(block, carry):
            start = pl.multiple_of(block * BLOCK, BLOCK)
            for channel in range(4):
                total[channel, :, pl.ds(start, BLOCK)] = jnp.full(
                    (band_rows, BLOCK), 0.0 if channel < 3 else 1.0, jnp.float32
                )
            return carry

        lax.fori_loop(0, blocks, clear, 0)

    def add(earlier, carry):
        shift = shear_rows[earlier]
        return carry[0] + rows_from_low(shift), carry[1] + rows_from_high(shift)

    def shear_slice(index, slot, used):
        row_shift = shear_rows[index]
        col_shift = shear_cols[index]
        low_count = rows_from_low(row_shift)
        high_count = rows_from_high(row_shift)
        low_start = groups * 8 - used[0] - low_count
        high_start = used[1]

        def premultiply(load, row, count):
            def body(block, carry):
                start = pl.multiple_of(block * BLOCK, BLOCK)
                opacity = load(3, start)
                for channel in range(4):
                    value = opacity
                    if channel < 3:
                        value = load(channel, start) * opacity
                    for half in range(BLOCK // 128):
                        premult[
                            block * (BLOCK // 128) + half, channel, pl.ds(row, count), :
                        ] = value[:, half * 128 : half * 128 + 128]
                return carry

            lax.fori_loop(0, columns // BLOCK, body, 0, unroll=PREMULT_UNROLL)

        @pl.when(index == begin)
        def _():
            for copy in copies:
                copy.wait()

        def rim_of(side, carry):
            packed_row = jnp.where(side == 0, low_start, high_start)
            group = jnp.minimum(packed_row // 8, groups - 2)
            place = jnp.where(side == 0, 16 - low_count, 16 + band_rows)
            for half in range(2):
                premultiply(
                    lambda channel, start: halo[
                        side, group + half, channel, :, pl.ds(start, BLOCK)
                    ].astype(jnp.float32),
                    place - (packed_row - group * 8) + 8 * half,
                    8,
                )
            return carry

        lax.fori_loop(
            jnp.where(low_count > 0, 0, 1), jnp.where(high_count > 0, 2, 1), rim_of, 0
        )
        premultiply(
            lambda channel, start: slabs[slot, channel, :, pl.ds(start, BLOCK)].astype(
                jnp.float32
            ),
            16,
            band_rows,
        )

        source = lax.broadcasted_iota(jnp.int32, (2 * BLOCK, BLOCK), 0)
        target = lax.broadcasted_iota(jnp.int32, (2 * BLOCK, BLOCK), 1)
        distance = jnp.abs(source - target - EDGE - col_shift)
        weights[...] = jnp.where(
            distance == 0, 0.125, jnp.where(distance == 1, 0.0625, 0.0)
        ).astype(jnp.bfloat16)

        def filter_rows(block, half, tile):
            for channel in range(4):
                first, middle, last = (
                    premult[tile, channel, pl.ds(16 + row_shift + shift, band_rows), :]
                    for shift in (-1, 0, 1)
                )
                bands[
                    block,
                    channel * band_rows : (channel + 1) * band_rows,
                    half * 128 : half * 128 + 128,
                ] = (first + last + (middle + middle)).astype(jnp.bfloat16)

        def filter_block(block, carry):
            for half in range(2):
                filter_rows(block, half, block * 2 - 1 + half)
            return carry

        filter_rows(0, 1, 0)
        filter_rows(blocks, 0, columns // 128 - 1)
        lax.fori_loop(1, blocks, filter_block, 0, unroll=ROW_UNROLL)

        def composite(step, carry):
            first = step * stacked
            here = bands[pl.ds(first, stacked)].reshape(stacked * 4 * band_rows, BLOCK)
            after = bands[pl.ds(first + 1, stacked)].reshape(stacked * 4 * band_rows, BLOCK)
            sheared = jnp.dot(
                here, weights[0:BLOCK, :], preferred_element_type=jnp.float32
            ) + jnp.dot(after, weights[BLOCK:, :], preferred_element_type=jnp.float32)
            for block in range(stacked):
                lanes = pl.ds(pl.multiple_of((first + block) * BLOCK, BLOCK), BLOCK)
                top = block * 4 * band_rows
                parts = [
                    sheared[top + channel * band_rows : top + (channel + 1) * band_rows]
                    for channel in range(4)
                ]
                passed = total[3, :, lanes]
                for channel in range(3):
                    total[channel, :, lanes] = total[channel, :, lanes] + passed * parts[channel]
                total[3, :, lanes] = passed - passed * parts[3]
            return carry

        lax.fori_loop(0, blocks // stacked, composite, 0)

    def one_slice(index, used):
        fetch(index).wait()

        @pl.when(index + DEPTH - 1 < end)
        def _():
            fetch(index + DEPTH - 1).start()

        shear_slice(index, lax.rem(index, DEPTH), used)
        return add(index, used)

    lax.fori_loop(begin, end, one_slice, lax.fori_loop(0, begin, add, (0, 0)))
    if part == "back":
        emit_tiles(total, bounds[2], kept_ref, sent_ref)


def emit_tiles(total, core, kept_ref, sent_ref):
    _, band_rows, columns = total.shape
    pairs = kept_ref.shape[0]
    width = columns // (2 * pairs)
    lane = lax.broadcasted_iota(jnp.int32, (band_rows, EDGE), 1)

    def value(channel, start, size):
        part = total[channel, :, pl.ds(pl.multiple_of(start, EDGE), size)]
        return part if channel < 3 else 1.0 - part

    def body(pair, carry):
        for tile, image_ref in ((2 * pair + core, kept_ref), (2 * pair + 1 - core, sent_ref)):
            first = tile * width
            for channel in range(4):
                image_ref[pair, channel, :, 0:width] = value(channel, first, width).astype(
                    jnp.bfloat16
                )
                before = value(channel, jnp.maximum(first - EDGE, 0), EDGE)
                after = value(channel, jnp.minimum(first + width, columns - EDGE), EDGE)
                before = jnp.where(tile > 0, before, 0.0)
                after = jnp.where(tile < 2 * pairs - 1, after, 0.0)
                image_ref[pair, channel, :, width:] = jnp.where(
                    lane < EDGE // 2, after, before
                ).astype(jnp.bfloat16)
        return carry

    lax.fori_loop(0, pairs, body, 0)


def shear_part(part, bounds, volume, shear_rows, shear_cols, packed, before, tiles):
    _, _, band_rows, columns = volume.shape
    groups = sum(chunk.shape[0] for chunk in packed) // 2

    outside = list(packed) + ([] if before is None else [before])
    total_shape = (4, band_rows, columns)
    scratch = [
        pltpu.VMEM((columns // 128, 4, band_rows + 32, 128), jnp.float32),
        pltpu.VMEM((columns // BLOCK + 1, 4 * band_rows, BLOCK), jnp.bfloat16),
        pltpu.VMEM((2 * BLOCK, BLOCK), jnp.bfloat16),
        pltpu.VMEM((2, groups, 4, 8, columns), jnp.bfloat16),
        pltpu.VMEM((DEPTH, 4, band_rows, columns), jnp.bfloat16),
        pltpu.SemaphoreType.DMA((len(outside),)),
        pltpu.SemaphoreType.DMA((DEPTH,)),
    ]
    if part == "front":
        outs = [jax.ShapeDtypeStruct(total_shape, jnp.float32)]
    else:
        image = (tiles // 2, 4, band_rows, columns // tiles + EDGE)
        outs = [jax.ShapeDtypeStruct(image, jnp.bfloat16)] * 2
        scratch.append(pltpu.VMEM(total_shape, jnp.float32))
    whole = len(outs[0].shape)
    return pl.pallas_call(
        functools.partial(shear_kernel, part),
        out_shape=outs,
        grid_spec=pltpu.PrefetchScalarGridSpec(
            num_scalar_prefetch=3,
            grid=(1,),
            in_specs=[pl.BlockSpec(memory_space=pl.ANY)] * (1 + len(outside)),
            out_specs=[
                pl.BlockSpec(
                    out.shape, lambda i, a, b, c: (0,) * whole, pipeline_mode=pl.Buffered(1)
                )
                for out in outs
            ],
            scratch_shapes=scratch,
        ),
        compiler_params=pltpu.CompilerParams(vmem_limit_bytes=VMEM_LIMIT),
        cost_estimate=pl.CostEstimate(
            flops=2 * 512 * volume.size, transcendentals=0, bytes_accessed=volume.size
        ),
    )(shear_rows, shear_cols, bounds, volume, *outside)


def weight_of(offset):
    return jnp.where(offset == 0, 0.5, jnp.where(jnp.abs(offset) == 1, 0.25, 0.0))


def across_kernel(pieces_ref, shifts_ref, across_ref, top_ref, bottom_ref):
    tiles, _, band_rows, padded = pieces_ref.shape
    width = across_ref.shape[2]
    for row in range(0, band_rows, 8):
        rows = slice(row, row + 8)
        totals = [None] * 4
        passed = None
        for tile in range(tiles):
            parts = [pieces_ref[tile, channel, rows, :].astype(jnp.float32) for channel in range(4)]
            if tile == 0:
                totals = parts[:3]
                passed = 1.0 - parts[3]
            else:
                totals = [total + passed * part for total, part in zip(totals, parts[:3])]
                passed = passed - passed * parts[3]
        totals = totals[:3] + [1.0 - passed]
        shifts = jnp.broadcast_to(shifts_ref[rows, :], (8, width))
        results = [jnp.zeros((8, width), jnp.float32)] * 4
        for offset in range(-RIM, RIM + 1):
            factor = weight_of(offset - shifts)
            for channel in range(4):
                moved = pltpu.roll(totals[channel], (-offset) % padded, 1)[:, :width]
                results[channel] = results[channel] + factor * moved
        for channel in range(4):
            across_ref[channel, rows, :] = results[channel]
    for channel in range(4):
        top_ref[channel * RIM : (channel + 1) * RIM, :] = across_ref[channel, 0:RIM, :]
        bottom_ref[channel * RIM : (channel + 1) * RIM, :] = across_ref[
            channel, band_rows - RIM : band_rows, :
        ]


def warp_columns(pieces, shifts, width):
    _, _, band_rows, _ = pieces.shape
    rim = jax.ShapeDtypeStruct((4 * RIM, width), jnp.float32)
    return pl.pallas_call(
        across_kernel,
        out_shape=(jax.ShapeDtypeStruct((4, band_rows, width), jnp.float32), rim, rim),
        compiler_params=pltpu.CompilerParams(vmem_limit_bytes=VMEM_LIMIT),
    )(pieces, shifts)


def final_kernel(across_ref, low_ref, high_ref, shifts_ref, final_ref, extended):
    _, band_rows, width = across_ref.shape
    for channel in range(4):
        extended[channel, 16 : 16 + band_rows, :] = across_ref[channel]
        rim = slice(channel * RIM, (channel + 1) * RIM)
        extended[channel, 16 - RIM : 16, :] = low_ref[rim, :]
        extended[channel, 16 + band_rows : 16 + band_rows + RIM, :] = high_ref[rim, :]
    for lane in range(0, width, 128):
        lanes = slice(lane, lane + 128)
        shifts = jnp.broadcast_to(shifts_ref[:, lanes], (8, 128))
        factors = [weight_of(offset - shifts) for offset in range(-RIM, RIM + 1)]
        for channel in range(4):
            for row in range(0, band_rows, 8):
                result = jnp.zeros((8, 128), jnp.float32)
                for offset in range(-RIM, RIM + 1):
                    start = 16 + row + offset
                    result = result + factors[offset + RIM] * extended[
                        channel, start : start + 8, lanes
                    ]
                final_ref[channel, row : row + 8, lanes] = result


def warp_rows_of(across, low, high, shifts):
    _, band_rows, width = across.shape
    return pl.pallas_call(
        final_kernel,
        out_shape=jax.ShapeDtypeStruct(across.shape, jnp.float32),
        scratch_shapes=[pltpu.VMEM((4, band_rows + 32, width), jnp.float32)],
        compiler_params=pltpu.CompilerParams(vmem_limit_bytes=VMEM_LIMIT),
    )(across, low, high, shifts)


def over_front(front_part, back_part):
    return front_part + (1.0 - front_part[:, 3:4]) * back_part


def neighbours(axis):
    count = lax.axis_size(axis)
    forward = [(i, i + 1) for i in range(count - 1)]
    return forward, [(target, source) for source, target in forward]


def per_device(volume, shear_rows, shear_cols, warp_cols, warp_rows):
    band_rows = volume.shape[2]
    columns = volume.shape[3]
    tiles = lax.axis_size("depth")
    width = columns // tiles
    core = lax.axis_index("depth") % 2
    forward, backward = neighbours("rows")
    slices = volume.shape[1]
    most = -(-RIM * slices // 8)
    sizes = [size for size in SIZES if size < most] + [most]
    earlier = jnp.arange(slices)[None, :] <= jnp.arange(slices)[:, None]
    reach = jnp.maximum(
        jnp.sum(jnp.where(earlier, rows_from_high(shear_rows)[None, :], 0), 1),
        jnp.sum(jnp.where(earlier, rows_from_low(shear_rows)[None, :], 0), 1),
    )
    needed = reach[slices - 1]
    choice = sum((needed > 8 * size).astype(jnp.int32) for size in sizes[:-1])

    def with_groups(groups):
        early = (groups + 1) // 2
        late = groups - early

        def branch(volume, shear_rows, shear_cols, reach):
            middle = jnp.minimum(jnp.sum((reach <= 8 * early).astype(jnp.int32)), slices - 1)
            begin, end = jnp.zeros_like(middle), jnp.full_like(middle, slices)
            up_first, down_first = pack_halo(volume, shear_rows, 0, early)
            up_second, down_second = pack_halo(volume, shear_rows, early, late)
            high_first = lax.ppermute(up_first, "rows", backward)
            low_first = lax.ppermute(down_first, "rows", forward)
            high_second = lax.ppermute(up_second, "rows", backward)
            low_second = lax.ppermute(down_second, "rows", forward)
            (total,) = shear_part(
                "front", jnp.stack([begin, middle]), volume, shear_rows, shear_cols,
                (low_first, high_first), None, tiles,
            )
            return shear_part(
                "back", jnp.stack([middle, end, core]), volume, shear_rows, shear_cols,
                (low_first, low_second, high_first, high_second), total, tiles,
            )

        return branch

    kept, sent = lax.switch(
        choice, [with_groups(groups) for groups in sizes], volume, shear_rows, shear_cols, reach
    )
    received = lax.ppermute(sent, "depth", [(i, i ^ 1) for i in range(tiles)])
    merged = over_front(
        jnp.where(core == 0, kept, received).astype(jnp.float32),
        jnp.where(core == 0, received, kept).astype(jnp.float32),
    ).astype(jnp.bfloat16)
    pieces = lax.all_to_all(
        merged, "depth", 0, 0, tiled=True,
        axis_index_groups=[list(range(first, tiles, 2)) for first in range(2)],
    )
    row_start = lax.axis_index("rows") * band_rows
    row_shifts = lax.dynamic_slice_in_dim(warp_cols, row_start, band_rows, 0)
    across, top, bottom = warp_columns(pieces, row_shifts[:, None], width)
    below = lax.ppermute(bottom, "rows", forward)
    above = lax.ppermute(top, "rows", backward)
    return warp_rows_of(across, below, above, warp_rows[None, :])


def solution(mesh):
    return jax.shard_map(
        per_device,
        mesh=mesh,
        in_specs=(P(None, "depth", "rows", None), P("depth"), P("depth"), P(), P("depth")),
        out_specs=P(None, "rows", "depth"),
        check_vma=False,
    )
```

```python
import functools

import jax
import jax.numpy as jnp
from jax import lax
from jax.experimental import pallas as pl
from jax.experimental.pallas import tpu as pltpu
from jax.sharding import PartitionSpec as P

SHIFT = 8
RIM = SHIFT + 1
BLOCK = 256
GROUP = 16
ROW_UNROLL = 3
PREMULT_UNROLL = 4
PACK_UNROLL = 8
DEPTH = 4
SIZES = (6, 7, 8, 9, 10, 12)
EDGE = 128
VMEM_LIMIT = 60 * 1024 * 1024


def rows_from_high(shift):
    return jnp.maximum(shift + 1, 0)


def rows_from_low(shift):
    return jnp.maximum(1 - shift, 0)


def pack_kernel(
    first_row, shear_rows, volume_ref, up_ref, down_ref,
    up_tiles, down_tiles, up_rows, down_rows, up_out, down_out, in_sems, out_sems,
):
    groups = up_ref.shape[0]
    slices = volume_ref.shape[1]
    band_rows = volume_ref.shape[2]
    tiles = up_ref.shape[3] // 128
    chunk_rows = groups * 8
    row_bufs = (up_rows, down_rows)

    def fetch(index, side, count):
        buffer = (up_tiles, down_tiles)[side]
        first = 0 if side == 0 else band_rows - count
        place = 0 if side == 0 else 16 - count
        return pltpu.make_async_copy(
            volume_ref.at[:, index, pl.ds(first, count), :],
            buffer.at[index, :, pl.ds(place, count), :],
            in_sems.at[side, index],
        )

    def each_size(needed, used, act):
        in_chunk = (used < first_row + chunk_rows) & (used + needed > first_row)

        @pl.when(in_chunk & (needed > 0) & (needed <= 8))
        def _():
            act(8)

        @pl.when(in_chunk & (needed > 8))
        def _():
            act(16)

    def scatter(index, side, count, row):
        fetch(index, side, count).wait()
        source = (up_tiles, down_tiles)[side]
        target = row_bufs[side]
        first = 0 if side == 0 else 16 - count

        def body(tile, carry):
            lane = pl.multiple_of(tile * 128, 128)
            for channel in range(4):
                target[tile, channel, pl.ds(row, count), :] = source[
                    index, channel, first : first + count, pl.ds(lane, 128)
                ].astype(jnp.float32)
            return carry

        lax.fori_loop(0, tiles, body, 0, unroll=PACK_UNROLL)

    def for_slices(act):
        def body(index, used):
            shift = shear_rows[index]
            counts = rows_from_high(shift), rows_from_low(shift)
            for side in range(2):
                each_size(counts[side], used[side], functools.partial(act, index, side, used[side]))
            return used[0] + counts[0], used[1] + counts[1]

        lax.fori_loop(0, slices, body, (0, 0))

    def start(index, side, used, count):
        fetch(index, side, count).start()

    def place(index, side, used, count):
        row = used - first_row + 16
        scatter(index, side, count, row if side == 0 else chunk_rows + 32 - row - count)

    for_slices(start)
    for_slices(place)

    def send(side, group):
        return pltpu.make_async_copy(
            (up_out, down_out)[side].at[group], (up_ref, down_ref)[side].at[group], out_sems.at[side, group]
        )

    def flush(group, carry):
        row = pl.multiple_of(group * 8 + 16, 8)
        for side, target in enumerate((up_out, down_out)):

            def body(tile, carry):
                lanes = pl.ds(pl.multiple_of(tile * 128, 128), 128)
                for channel in range(4):
                    target[group, channel, :, lanes] = row_bufs[side][
                        tile, channel, pl.ds(row, 8), :
                    ].astype(jnp.bfloat16)
                return carry

            lax.fori_loop(0, tiles, body, 0, unroll=PACK_UNROLL)
            send(side, group).start()
        return carry

    def finish(group, carry):
        for side in range(2):
            send(side, group).wait()
        return carry

    lax.fori_loop(0, groups, flush, 0)
    lax.fori_loop(0, groups, finish, 0)


def pack_halo(volume, shear_rows, first, groups):
    _, slices, _, columns = volume.shape
    packed = jax.ShapeDtypeStruct((groups, 4, 8, columns), jnp.bfloat16)
    tiles = pltpu.VMEM((slices, 4, 16, columns), jnp.bfloat16)
    rows = pltpu.VMEM((columns // 128, 4, groups * 8 + 32, 128), jnp.float32)
    out = pltpu.VMEM((groups, 4, 8, columns), jnp.bfloat16)
    return pl.pallas_call(
        functools.partial(pack_kernel, first * 8),
        out_shape=(packed, packed),
        grid_spec=pltpu.PrefetchScalarGridSpec(
            num_scalar_prefetch=1,
            grid=(1,),
            in_specs=[pl.BlockSpec(memory_space=pl.ANY)],
            out_specs=[pl.BlockSpec(memory_space=pl.ANY)] * 2,
            scratch_shapes=[
                tiles, tiles, rows, rows, out, out,
                pltpu.SemaphoreType.DMA((2, slices)),
                pltpu.SemaphoreType.DMA((2, groups)),
            ],
        ),
        compiler_params=pltpu.CompilerParams(vmem_limit_bytes=VMEM_LIMIT),
        cost_estimate=pl.CostEstimate(
            flops=volume.size // 16, transcendentals=0, bytes_accessed=volume.size // 4
        ),
    )(shear_rows, volume)


def shear_kernel(part, *refs):
    shear_rows, shear_cols, bounds, volume_ref = refs[:4]
    if part == "front":
        low_refs, high_refs = [refs[4]], [refs[5]]
        before_ref, total, premult, bands, weights, halo, slabs, sems, slab_sems = None, *refs[6:]
    else:
        low_refs, high_refs = [refs[5], refs[4]], [refs[6], refs[7]]
        before_ref, kept_ref, sent_ref, premult, bands, weights, halo, slabs, sems, slab_sems, total = refs[8:]
    begin = bounds[0]
    end = bounds[1]
    band_rows = volume_ref.shape[2]
    columns = volume_ref.shape[3]
    blocks = columns // BLOCK
    groups = halo.shape[1]
    stacked = min(GROUP, blocks)

    def fetch(index):
        slot = lax.rem(index, DEPTH)
        return pltpu.make_async_copy(volume_ref.at[:, index], slabs.at[slot], slab_sems.at[slot])

    copies = []
    for side, packed in enumerate((low_refs, high_refs)):
        first = 0
        for ref in packed:
            count = ref.shape[0]
            copies.append((ref, halo.at[side, pl.ds(first, count)]))
            first += count
    if before_ref is not None:
        copies.append((before_ref, total))
    copies = [
        pltpu.make_async_copy(source, target, sems.at[place])
        for place, (source, target) in enumerate(copies)
    ]

    for ahead in range(DEPTH - 1):

        @pl.when(begin + ahead < end)
        def _():
            fetch(begin + ahead).start()

    for copy in copies:
        copy.start()
    none = jnp.zeros((bands.shape[1], EDGE), jnp.bfloat16)
    bands[0, :, 0:EDGE] = none
    bands[blocks, :, EDGE:] = none
    if before_ref is None:

        def clear(block, carry):
            start = pl.multiple_of(block * BLOCK, BLOCK)
            for channel in range(4):
                total[channel, :, pl.ds(start, BLOCK)] = jnp.full(
                    (band_rows, BLOCK), 0.0 if channel < 3 else 1.0, jnp.float32
                )
            return carry

        lax.fori_loop(0, blocks, clear, 0)

    def add(earlier, carry):
        shift = shear_rows[earlier]
        return carry[0] + rows_from_low(shift), carry[1] + rows_from_high(shift)

    def shear_slice(index, slot, used):
        row_shift = shear_rows[index]
        col_shift = shear_cols[index]
        low_count = rows_from_low(row_shift)
        high_count = rows_from_high(row_shift)
        low_start = groups * 8 - used[0] - low_count
        high_start = used[1]

        def premultiply(load, row, count):
            def body(block, carry):
                start = pl.multiple_of(block * BLOCK, BLOCK)
                opacity = load(3, start)
                for channel in range(4):
                    value = opacity
                    if channel < 3:
                        value = load(channel, start) * opacity
                    for half in range(BLOCK // 128):
                        premult[
                            block * (BLOCK // 128) + half, channel, pl.ds(row, count), :
                        ] = value[:, half * 128 : half * 128 + 128]
                return carry

            lax.fori_loop(0, columns // BLOCK, body, 0, unroll=PREMULT_UNROLL)

        @pl.when(index == begin)
        def _():
            for copy in copies:
                copy.wait()

        def rim_of(side, carry):
            packed_row = jnp.where(side == 0, low_start, high_start)
            group = jnp.minimum(packed_row // 8, groups - 2)
            place = jnp.where(side == 0, 16 - low_count, 16 + band_rows)
            for half in range(2):
                premultiply(
                    lambda channel, start: halo[
                        side, group + half, channel, :, pl.ds(start, BLOCK)
                    ].astype(jnp.float32),
                    place - (packed_row - group * 8) + 8 * half,
                    8,
                )
            return carry

        lax.fori_loop(
            jnp.where(low_count > 0, 0, 1), jnp.where(high_count > 0, 2, 1), rim_of, 0
        )
        premultiply(
            lambda channel, start: slabs[slot, channel, :, pl.ds(start, BLOCK)].astype(
                jnp.float32
            ),
            16,
            band_rows,
        )

        source = lax.broadcasted_iota(jnp.int32, (2 * BLOCK, BLOCK), 0)
        target = lax.broadcasted_iota(jnp.int32, (2 * BLOCK, BLOCK), 1)
        distance = jnp.abs(source - target - EDGE - col_shift)
        weights[...] = jnp.where(
            distance == 0, 0.125, jnp.where(distance == 1, 0.0625, 0.0)
        ).astype(jnp.bfloat16)

        def filter_rows(block, half, tile):
            for channel in range(4):
                first, middle, last = (
                    premult[tile, channel, pl.ds(16 + row_shift + shift, band_rows), :]
                    for shift in (-1, 0, 1)
                )
                bands[
                    block,
                    channel * band_rows : (channel + 1) * band_rows,
                    half * 128 : half * 128 + 128,
                ] = (first + last + (middle + middle)).astype(jnp.bfloat16)

        def filter_block(block, carry):
            for half in range(2):
                filter_rows(block, half, block * 2 - 1 + half)
            return carry

        filter_rows(0, 1, 0)
        filter_rows(blocks, 0, columns // 128 - 1)
        lax.fori_loop(1, blocks, filter_block, 0, unroll=ROW_UNROLL)

        def composite(step, carry):
            first = step * stacked
            here = bands[pl.ds(first, stacked)].reshape(stacked * 4 * band_rows, BLOCK)
            after = bands[pl.ds(first + 1, stacked)].reshape(stacked * 4 * band_rows, BLOCK)
            sheared = jnp.dot(
                here, weights[0:BLOCK, :], preferred_element_type=jnp.float32
            ) + jnp.dot(after, weights[BLOCK:, :], preferred_element_type=jnp.float32)
            for block in range(stacked):
                lanes = pl.ds(pl.multiple_of((first + block) * BLOCK, BLOCK), BLOCK)
                top = block * 4 * band_rows
                parts = [
                    sheared[top + channel * band_rows : top + (channel + 1) * band_rows]
                    for channel in range(4)
                ]
                passed = total[3, :, lanes]
                for channel in range(3):
                    total[channel, :, lanes] = total[channel, :, lanes] + passed * parts[channel]
                total[3, :, lanes] = passed - passed * parts[3]
            return carry

        lax.fori_loop(0, blocks // stacked, composite, 0)

    def one_slice(index, used):
        fetch(index).wait()

        @pl.when(index + DEPTH - 1 < end)
        def _():
            fetch(index + DEPTH - 1).start()

        shear_slice(index, lax.rem(index, DEPTH), used)
        return add(index, used)

    lax.fori_loop(begin, end, one_slice, lax.fori_loop(0, begin, add, (0, 0)))
    if part == "back":
        emit_tiles(total, bounds[2], kept_ref, sent_ref)


def emit_tiles(total, core, kept_ref, sent_ref):
    _, band_rows, columns = total.shape
    pairs = kept_ref.shape[0]
    width = columns // (2 * pairs)
    lane = lax.broadcasted_iota(jnp.int32, (band_rows, EDGE), 1)

    def value(channel, start, size):
        part = total[channel, :, pl.ds(pl.multiple_of(start, EDGE), size)]
        return part if channel < 3 else 1.0 - part

    def body(pair, carry):
        for tile, image_ref in ((2 * pair + core, kept_ref), (2 * pair + 1 - core, sent_ref)):
            first = tile * width
            for channel in range(4):
                image_ref[pair, channel, :, 0:width] = value(channel, first, width).astype(
                    jnp.bfloat16
                )
                before = value(channel, jnp.maximum(first - EDGE, 0), EDGE)
                after = value(channel, jnp.minimum(first + width, columns - EDGE), EDGE)
                before = jnp.where(tile > 0, before, 0.0)
                after = jnp.where(tile < 2 * pairs - 1, after, 0.0)
                image_ref[pair, channel, :, width:] = jnp.where(
                    lane < EDGE // 2, after, before
                ).astype(jnp.bfloat16)
        return carry

    lax.fori_loop(0, pairs, body, 0)


def shear_part(part, bounds, volume, shear_rows, shear_cols, packed, before, tiles):
    _, _, band_rows, columns = volume.shape
    groups = sum(chunk.shape[0] for chunk in packed) // 2

    outside = list(packed) + ([] if before is None else [before])
    total_shape = (4, band_rows, columns)
    scratch = [
        pltpu.VMEM((columns // 128, 4, band_rows + 32, 128), jnp.float32),
        pltpu.VMEM((columns // BLOCK + 1, 4 * band_rows, BLOCK), jnp.bfloat16),
        pltpu.VMEM((2 * BLOCK, BLOCK), jnp.bfloat16),
        pltpu.VMEM((2, groups, 4, 8, columns), jnp.bfloat16),
        pltpu.VMEM((DEPTH, 4, band_rows, columns), jnp.bfloat16),
        pltpu.SemaphoreType.DMA((len(outside),)),
        pltpu.SemaphoreType.DMA((DEPTH,)),
    ]
    if part == "front":
        outs = [jax.ShapeDtypeStruct(total_shape, jnp.float32)]
    else:
        image = (tiles // 2, 4, band_rows, columns // tiles + EDGE)
        outs = [jax.ShapeDtypeStruct(image, jnp.bfloat16)] * 2
        scratch.append(pltpu.VMEM(total_shape, jnp.float32))
    whole = len(outs[0].shape)
    return pl.pallas_call(
        functools.partial(shear_kernel, part),
        out_shape=outs,
        grid_spec=pltpu.PrefetchScalarGridSpec(
            num_scalar_prefetch=3,
            grid=(1,),
            in_specs=[pl.BlockSpec(memory_space=pl.ANY)] * (1 + len(outside)),
            out_specs=[
                pl.BlockSpec(
                    out.shape, lambda i, a, b, c: (0,) * whole, pipeline_mode=pl.Buffered(1)
                )
                for out in outs
            ],
            scratch_shapes=scratch,
        ),
        compiler_params=pltpu.CompilerParams(vmem_limit_bytes=VMEM_LIMIT),
        cost_estimate=pl.CostEstimate(
            flops=2 * 512 * volume.size, transcendentals=0, bytes_accessed=volume.size
        ),
    )(shear_rows, shear_cols, bounds, volume, *outside)


def weight_of(offset):
    return jnp.where(offset == 0, 0.5, jnp.where(jnp.abs(offset) == 1, 0.25, 0.0))


def across_kernel(pieces_ref, shifts_ref, across_ref, top_ref, bottom_ref):
    tiles, _, band_rows, padded = pieces_ref.shape
    width = across_ref.shape[2]
    for row in range(0, band_rows, 8):
        rows = slice(row, row + 8)
        totals = [None] * 4
        passed = None
        for tile in range(tiles):
            parts = [pieces_ref[tile, channel, rows, :].astype(jnp.float32) for channel in range(4)]
            if tile == 0:
                totals = parts[:3]
                passed = 1.0 - parts[3]
            else:
                totals = [total + passed * part for total, part in zip(totals, parts[:3])]
                passed = passed - passed * parts[3]
        totals = totals[:3] + [1.0 - passed]
        shifts = jnp.broadcast_to(shifts_ref[rows, :], (8, width))
        results = [jnp.zeros((8, width), jnp.float32)] * 4
        for offset in range(-RIM, RIM + 1):
            factor = weight_of(offset - shifts)
            for channel in range(4):
                moved = pltpu.roll(totals[channel], (-offset) % padded, 1)[:, :width]
                results[channel] = results[channel] + factor * moved
        for channel in range(4):
            across_ref[channel, rows, :] = results[channel]
    for channel in range(4):
        top_ref[channel * RIM : (channel + 1) * RIM, :] = across_ref[channel, 0:RIM, :]
        bottom_ref[channel * RIM : (channel + 1) * RIM, :] = across_ref[
            channel, band_rows - RIM : band_rows, :
        ]


def warp_columns(pieces, shifts, width):
    _, _, band_rows, _ = pieces.shape
    rim = jax.ShapeDtypeStruct((4 * RIM, width), jnp.float32)
    return pl.pallas_call(
        across_kernel,
        out_shape=(jax.ShapeDtypeStruct((4, band_rows, width), jnp.float32), rim, rim),
        compiler_params=pltpu.CompilerParams(vmem_limit_bytes=VMEM_LIMIT),
    )(pieces, shifts)


def final_kernel(across_ref, low_ref, high_ref, shifts_ref, final_ref, extended):
    _, band_rows, width = across_ref.shape
    for channel in range(4):
        extended[channel, 16 : 16 + band_rows, :] = across_ref[channel]
        rim = slice(channel * RIM, (channel + 1) * RIM)
        extended[channel, 16 - RIM : 16, :] = low_ref[rim, :]
        extended[channel, 16 + band_rows : 16 + band_rows + RIM, :] = high_ref[rim, :]
    for lane in range(0, width, 128):
        lanes = slice(lane, lane + 128)
        shifts = jnp.broadcast_to(shifts_ref[:, lanes], (8, 128))
        factors = [weight_of(offset - shifts) for offset in range(-RIM, RIM + 1)]
        for channel in range(4):
            for row in range(0, band_rows, 8):
                result = jnp.zeros((8, 128), jnp.float32)
                for offset in range(-RIM, RIM + 1):
                    start = 16 + row + offset
                    result = result + factors[offset + RIM] * extended[
                        channel, start : start + 8, lanes
                    ]
                final_ref[channel, row : row + 8, lanes] = result


def warp_rows_of(across, low, high, shifts):
    _, band_rows, width = across.shape
    return pl.pallas_call(
        final_kernel,
        out_shape=jax.ShapeDtypeStruct(across.shape, jnp.float32),
        scratch_shapes=[pltpu.VMEM((4, band_rows + 32, width), jnp.float32)],
        compiler_params=pltpu.CompilerParams(vmem_limit_bytes=VMEM_LIMIT),
    )(across, low, high, shifts)


def over_front(front_part, back_part):
    return front_part + (1.0 - front_part[:, 3:4]) * back_part


def neighbours(axis):
    count = lax.axis_size(axis)
    forward = [(i, i + 1) for i in range(count - 1)]
    return forward, [(target, source) for source, target in forward]


def per_device(volume, shear_rows, shear_cols, warp_cols, warp_rows):
    band_rows = volume.shape[2]
    columns = volume.shape[3]
    tiles = lax.axis_size("depth")
    width = columns // tiles
    core = lax.axis_index("depth") % 2
    forward, backward = neighbours("rows")
    slices = volume.shape[1]
    most = -(-RIM * slices // 8)
    sizes = [size for size in SIZES if size < most] + [most]
    earlier = jnp.arange(slices)[None, :] <= jnp.arange(slices)[:, None]
    reach = jnp.maximum(
        jnp.sum(jnp.where(earlier, rows_from_high(shear_rows)[None, :], 0), 1),
        jnp.sum(jnp.where(earlier, rows_from_low(shear_rows)[None, :], 0), 1),
    )
    needed = jnp.maximum(
        jnp.sum(rows_from_high(shear_rows)), jnp.sum(rows_from_low(shear_rows))
    )
    choice = sum((needed > 8 * size).astype(jnp.int32) for size in sizes[:-1])

    def with_groups(groups):
        early = groups * 3 // 7
        late = groups - early

        def branch(volume, shear_rows, shear_cols, reach):
            middle = jnp.minimum(jnp.sum((reach <= 8 * early).astype(jnp.int32)), slices - 1)
            begin, end = jnp.zeros_like(middle), jnp.full_like(middle, slices)
            up_first, down_first = pack_halo(volume, shear_rows, 0, early)
            up_second, down_second = pack_halo(volume, shear_rows, early, late)
            high_first = lax.ppermute(up_first, "rows", backward)
            low_first = lax.ppermute(down_first, "rows", forward)
            high_second = lax.ppermute(up_second, "rows", backward)
            low_second = lax.ppermute(down_second, "rows", forward)
            (total,) = shear_part(
                "front", jnp.stack([begin, middle]), volume, shear_rows, shear_cols,
                (low_first, high_first), None, tiles,
            )
            return shear_part(
                "back", jnp.stack([middle, end, core]), volume, shear_rows, shear_cols,
                (low_first, low_second, high_first, high_second), total, tiles,
            )

        return branch

    kept, sent = lax.switch(
        choice, [with_groups(groups) for groups in sizes], volume, shear_rows, shear_cols, reach
    )
    received = lax.ppermute(sent, "depth", [(i, i ^ 1) for i in range(tiles)])
    merged = over_front(
        jnp.where(core == 0, kept, received).astype(jnp.float32),
        jnp.where(core == 0, received, kept).astype(jnp.float32),
    ).astype(jnp.bfloat16)
    pieces = lax.all_to_all(
        merged, "depth", 0, 0, tiled=True,
        axis_index_groups=[list(range(first, tiles, 2)) for first in range(2)],
    )
    row_start = lax.axis_index("rows") * band_rows
    row_shifts = lax.dynamic_slice_in_dim(warp_cols, row_start, band_rows, 0)
    across, top, bottom = warp_columns(pieces, row_shifts[:, None], width)
    below = lax.ppermute(bottom, "rows", forward)
    above = lax.ppermute(top, "rows", backward)
    return warp_rows_of(across, below, above, warp_rows[None, :])


def solution(mesh):
    return jax.shard_map(
        per_device,
        mesh=mesh,
        in_specs=(P(None, "depth", "rows", None), P("depth"), P("depth"), P(), P("depth")),
        out_specs=P(None, "rows", "depth"),
        check_vma=False,
    )
```

```python
import functools

import jax
import jax.numpy as jnp
from jax import lax
from jax.experimental import pallas as pl
from jax.experimental.pallas import tpu as pltpu
from jax.sharding import PartitionSpec as P

SHIFT = 8
RIM = SHIFT + 1
BLOCK = 256
GROUP = 16
ROW_UNROLL = 3
PREMULT_UNROLL = 4
PACK_UNROLL = 8
DEPTH = 3
SIZES = (6, 7, 8, 9, 10, 12)
EDGE = 128
VMEM_LIMIT = 60 * 1024 * 1024


def rows_from_high(shift):
    return jnp.maximum(shift + 1, 0)


def rows_from_low(shift):
    return jnp.maximum(1 - shift, 0)


def pack_kernel(
    first_row, shear_rows, volume_ref, up_ref, down_ref,
    up_tiles, down_tiles, up_rows, down_rows, up_out, down_out, in_sems, out_sems,
):
    groups = up_ref.shape[0]
    slices = volume_ref.shape[1]
    band_rows = volume_ref.shape[2]
    tiles = up_ref.shape[3] // 128
    chunk_rows = groups * 8
    row_bufs = (up_rows, down_rows)

    def fetch(index, side, count):
        buffer = (up_tiles, down_tiles)[side]
        first = 0 if side == 0 else band_rows - count
        place = 0 if side == 0 else 16 - count
        return pltpu.make_async_copy(
            volume_ref.at[:, index, pl.ds(first, count), :],
            buffer.at[index, :, pl.ds(place, count), :],
            in_sems.at[side, index],
        )

    def each_size(needed, used, act):
        in_chunk = (used < first_row + chunk_rows) & (used + needed > first_row)

        @pl.when(in_chunk & (needed > 0) & (needed <= 8))
        def _():
            act(8)

        @pl.when(in_chunk & (needed > 8))
        def _():
            act(16)

    def scatter(index, side, count, row):
        fetch(index, side, count).wait()
        source = (up_tiles, down_tiles)[side]
        target = row_bufs[side]
        first = 0 if side == 0 else 16 - count

        def body(tile, carry):
            lane = pl.multiple_of(tile * 128, 128)
            for channel in range(4):
                target[tile, channel, pl.ds(row, count), :] = source[
                    index, channel, first : first + count, pl.ds(lane, 128)
                ].astype(jnp.float32)
            return carry

        lax.fori_loop(0, tiles, body, 0, unroll=PACK_UNROLL)

    def for_slices(act):
        def body(index, used):
            shift = shear_rows[index]
            counts = rows_from_high(shift), rows_from_low(shift)
            for side in range(2):
                each_size(counts[side], used[side], functools.partial(act, index, side, used[side]))
            return used[0] + counts[0], used[1] + counts[1]

        lax.fori_loop(0, slices, body, (0, 0))

    def start(index, side, used, count):
        fetch(index, side, count).start()

    def place(index, side, used, count):
        row = used - first_row + 16
        scatter(index, side, count, row if side == 0 else chunk_rows + 32 - row - count)

    for_slices(start)
    for_slices(place)

    def send(side, group):
        return pltpu.make_async_copy(
            (up_out, down_out)[side].at[group], (up_ref, down_ref)[side].at[group], out_sems.at[side, group]
        )

    def flush(group, carry):
        row = pl.multiple_of(group * 8 + 16, 8)
        for side, target in enumerate((up_out, down_out)):

            def body(tile, carry):
                lanes = pl.ds(pl.multiple_of(tile * 128, 128), 128)
                for channel in range(4):
                    target[group, channel, :, lanes] = row_bufs[side][
                        tile, channel, pl.ds(row, 8), :
                    ].astype(jnp.bfloat16)
                return carry

            lax.fori_loop(0, tiles, body, 0, unroll=PACK_UNROLL)
            send(side, group).start()
        return carry

    def finish(group, carry):
        for side in range(2):
            send(side, group).wait()
        return carry

    lax.fori_loop(0, groups, flush, 0)
    lax.fori_loop(0, groups, finish, 0)


def pack_halo(volume, shear_rows, first, groups):
    _, slices, _, columns = volume.shape
    packed = jax.ShapeDtypeStruct((groups, 4, 8, columns), jnp.bfloat16)
    tiles = pltpu.VMEM((slices, 4, 16, columns), jnp.bfloat16)
    rows = pltpu.VMEM((columns // 128, 4, groups * 8 + 32, 128), jnp.float32)
    out = pltpu.VMEM((groups, 4, 8, columns), jnp.bfloat16)
    return pl.pallas_call(
        functools.partial(pack_kernel, first * 8),
        out_shape=(packed, packed),
        grid_spec=pltpu.PrefetchScalarGridSpec(
            num_scalar_prefetch=1,
            grid=(1,),
            in_specs=[pl.BlockSpec(memory_space=pl.ANY)],
            out_specs=[pl.BlockSpec(memory_space=pl.ANY)] * 2,
            scratch_shapes=[
                tiles, tiles, rows, rows, out, out,
                pltpu.SemaphoreType.DMA((2, slices)),
                pltpu.SemaphoreType.DMA((2, groups)),
            ],
        ),
        compiler_params=pltpu.CompilerParams(vmem_limit_bytes=VMEM_LIMIT),
        cost_estimate=pl.CostEstimate(
            flops=volume.size // 16, transcendentals=0, bytes_accessed=volume.size // 4
        ),
    )(shear_rows, volume)


def shear_kernel(part, *refs):
    shear_rows, shear_cols, bounds, volume_ref = refs[:4]
    if part == "front":
        low_refs, high_refs = [refs[4]], [refs[5]]
        before_ref, total, premult, bands, weights, halo, slabs, sems, slab_sems = None, *refs[6:]
    else:
        low_refs, high_refs = [refs[5], refs[4]], [refs[6], refs[7]]
        before_ref, kept_ref, sent_ref, premult, bands, weights, halo, slabs, sems, slab_sems, total = refs[8:]
    begin = bounds[0]
    end = bounds[1]
    band_rows = volume_ref.shape[2]
    columns = volume_ref.shape[3]
    blocks = columns // BLOCK
    groups = halo.shape[1]
    stacked = min(GROUP, blocks)

    def fetch(index):
        slot = lax.rem(index, DEPTH)
        return pltpu.make_async_copy(volume_ref.at[:, index], slabs.at[slot], slab_sems.at[slot])

    copies = []
    for side, packed in enumerate((low_refs, high_refs)):
        first = 0
        for ref in packed:
            count = ref.shape[0]
            copies.append((ref, halo.at[side, pl.ds(first, count)]))
            first += count
    if before_ref is not None:
        copies.append((before_ref, total))
    copies = [
        pltpu.make_async_copy(source, target, sems.at[place])
        for place, (source, target) in enumerate(copies)
    ]

    for ahead in range(DEPTH - 1):

        @pl.when(begin + ahead < end)
        def _():
            fetch(begin + ahead).start()

    for copy in copies:
        copy.start()
    none = jnp.zeros((bands.shape[1], EDGE), jnp.bfloat16)
    bands[0, :, 0:EDGE] = none
    bands[blocks, :, EDGE:] = none
    if before_ref is None:

        def clear(block, carry):
            start = pl.multiple_of(block * BLOCK, BLOCK)
            for channel in range(4):
                total[channel, :, pl.ds(start, BLOCK)] = jnp.full(
                    (band_rows, BLOCK), 0.0 if channel < 3 else 1.0, jnp.float32
                )
            return carry

        lax.fori_loop(0, blocks, clear, 0)

    def add(earlier, carry):
        shift = shear_rows[earlier]
        return carry[0] + rows_from_low(shift), carry[1] + rows_from_high(shift)

    def shear_slice(index, slot, used):
        row_shift = shear_rows[index]
        col_shift = shear_cols[index]
        low_count = rows_from_low(row_shift)
        high_count = rows_from_high(row_shift)
        low_start = groups * 8 - used[0] - low_count
        high_start = used[1]

        def premultiply(load, row, count):
            def body(block, carry):
                start = pl.multiple_of(block * BLOCK, BLOCK)
                opacity = load(3, start)
                for channel in range(4):
                    value = opacity
                    if channel < 3:
                        value = load(channel, start) * opacity
                    for half in range(BLOCK // 128):
                        premult[
                            block * (BLOCK // 128) + half, channel, pl.ds(row, count), :
                        ] = value[:, half * 128 : half * 128 + 128]
                return carry

            lax.fori_loop(0, columns // BLOCK, body, 0, unroll=PREMULT_UNROLL)

        @pl.when(index == begin)
        def _():
            for copy in copies:
                copy.wait()

        def rim_of(side, carry):
            packed_row = jnp.where(side == 0, low_start, high_start)
            count = jnp.where(side == 0, low_count, high_count)
            group = packed_row // 8
            ahead = packed_row - group * 8
            place = jnp.where(side == 0, 16 - low_count, 16 + band_rows) - ahead

            def one_group(half, carry):
                premultiply(
                    lambda channel, start: halo[
                        side, group + half, channel, :, pl.ds(start, BLOCK)
                    ].astype(jnp.float32),
                    place + 8 * half,
                    8,
                )
                return carry

            lax.fori_loop(0, jnp.where(ahead + count > 8, 2, 1), one_group, 0)
            return carry

        lax.fori_loop(
            jnp.where(low_count > 0, 0, 1), jnp.where(high_count > 0, 2, 1), rim_of, 0
        )
        premultiply(
            lambda channel, start: slabs[slot, channel, :, pl.ds(start, BLOCK)].astype(
                jnp.float32
            ),
            16,
            band_rows,
        )

        source = lax.broadcasted_iota(jnp.int32, (2 * BLOCK, BLOCK), 0)
        target = lax.broadcasted_iota(jnp.int32, (2 * BLOCK, BLOCK), 1)
        distance = jnp.abs(source - target - EDGE - col_shift)
        weights[...] = jnp.where(
            distance == 0, 0.125, jnp.where(distance == 1, 0.0625, 0.0)
        ).astype(jnp.bfloat16)

        def filter_rows(block, half, tile):
            for channel in range(4):
                first, middle, last = (
                    premult[tile, channel, pl.ds(16 + row_shift + shift, band_rows), :]
                    for shift in (-1, 0, 1)
                )
                bands[
                    block,
                    channel * band_rows : (channel + 1) * band_rows,
                    half * 128 : half * 128 + 128,
                ] = (first + last + (middle + middle)).astype(jnp.bfloat16)

        def filter_block(block, carry):
            for half in range(2):
                filter_rows(block, half, block * 2 - 1 + half)
            return carry

        filter_rows(0, 1, 0)
        filter_rows(blocks, 0, columns // 128 - 1)
        lax.fori_loop(1, blocks, filter_block, 0, unroll=ROW_UNROLL)

        def composite(step, carry):
            first = step * stacked
            here = bands[pl.ds(first, stacked)].reshape(stacked * 4 * band_rows, BLOCK)
            after = bands[pl.ds(first + 1, stacked)].reshape(stacked * 4 * band_rows, BLOCK)
            sheared = jnp.dot(
                here, weights[0:BLOCK, :], preferred_element_type=jnp.float32
            ) + jnp.dot(after, weights[BLOCK:, :], preferred_element_type=jnp.float32)
            for block in range(stacked):
                lanes = pl.ds(pl.multiple_of((first + block) * BLOCK, BLOCK), BLOCK)
                top = block * 4 * band_rows
                parts = [
                    sheared[top + channel * band_rows : top + (channel + 1) * band_rows]
                    for channel in range(4)
                ]
                passed = total[3, :, lanes]
                for channel in range(3):
                    total[channel, :, lanes] = total[channel, :, lanes] + passed * parts[channel]
                total[3, :, lanes] = passed - passed * parts[3]
            return carry

        lax.fori_loop(0, blocks // stacked, composite, 0)

    def one_slice(index, used):
        fetch(index).wait()

        @pl.when(index + DEPTH - 1 < end)
        def _():
            fetch(index + DEPTH - 1).start()

        shear_slice(index, lax.rem(index, DEPTH), used)
        return add(index, used)

    lax.fori_loop(begin, end, one_slice, lax.fori_loop(0, begin, add, (0, 0)))
    if part == "back":
        emit_tiles(total, bounds[2], kept_ref, sent_ref)


def emit_tiles(total, core, kept_ref, sent_ref):
    _, band_rows, columns = total.shape
    pairs = kept_ref.shape[0]
    width = columns // (2 * pairs)
    lane = lax.broadcasted_iota(jnp.int32, (band_rows, EDGE), 1)

    def value(channel, start, size):
        part = total[channel, :, pl.ds(pl.multiple_of(start, EDGE), size)]
        return part if channel < 3 else 1.0 - part

    def body(pair, carry):
        for tile, image_ref in ((2 * pair + core, kept_ref), (2 * pair + 1 - core, sent_ref)):
            first = tile * width
            for channel in range(4):
                image_ref[pair, channel, :, 0:width] = value(channel, first, width).astype(
                    jnp.bfloat16
                )
                before = value(channel, jnp.maximum(first - EDGE, 0), EDGE)
                after = value(channel, jnp.minimum(first + width, columns - EDGE), EDGE)
                before = jnp.where(tile > 0, before, 0.0)
                after = jnp.where(tile < 2 * pairs - 1, after, 0.0)
                image_ref[pair, channel, :, width:] = jnp.where(
                    lane < EDGE // 2, after, before
                ).astype(jnp.bfloat16)
        return carry

    lax.fori_loop(0, pairs, body, 0)


def shear_part(part, bounds, volume, shear_rows, shear_cols, packed, before, tiles):
    _, _, band_rows, columns = volume.shape
    groups = sum(chunk.shape[0] for chunk in packed) // 2

    outside = list(packed) + ([] if before is None else [before])
    total_shape = (4, band_rows, columns)
    scratch = [
        pltpu.VMEM((columns // 128, 4, band_rows + 32, 128), jnp.float32),
        pltpu.VMEM((columns // BLOCK + 1, 4 * band_rows, BLOCK), jnp.bfloat16),
        pltpu.VMEM((2 * BLOCK, BLOCK), jnp.bfloat16),
        pltpu.VMEM((2, groups, 4, 8, columns), jnp.bfloat16),
        pltpu.VMEM((DEPTH, 4, band_rows, columns), jnp.bfloat16),
        pltpu.SemaphoreType.DMA((len(outside),)),
        pltpu.SemaphoreType.DMA((DEPTH,)),
    ]
    if part == "front":
        outs = [jax.ShapeDtypeStruct(total_shape, jnp.float32)]
    else:
        image = (tiles // 2, 4, band_rows, columns // tiles + EDGE)
        outs = [jax.ShapeDtypeStruct(image, jnp.bfloat16)] * 2
        scratch.append(pltpu.VMEM(total_shape, jnp.float32))
    whole = len(outs[0].shape)
    return pl.pallas_call(
        functools.partial(shear_kernel, part),
        out_shape=outs,
        grid_spec=pltpu.PrefetchScalarGridSpec(
            num_scalar_prefetch=3,
            grid=(1,),
            in_specs=[pl.BlockSpec(memory_space=pl.ANY)] * (1 + len(outside)),
            out_specs=[
                pl.BlockSpec(
                    out.shape, lambda i, a, b, c: (0,) * whole, pipeline_mode=pl.Buffered(1)
                )
                for out in outs
            ],
            scratch_shapes=scratch,
        ),
        compiler_params=pltpu.CompilerParams(vmem_limit_bytes=VMEM_LIMIT),
        cost_estimate=pl.CostEstimate(
            flops=2 * 512 * volume.size, transcendentals=0, bytes_accessed=volume.size
        ),
    )(shear_rows, shear_cols, bounds, volume, *outside)


def weight_of(offset):
    return jnp.where(offset == 0, 0.5, jnp.where(jnp.abs(offset) == 1, 0.25, 0.0))


def across_kernel(pieces_ref, shifts_ref, across_ref, top_ref, bottom_ref):
    tiles, _, band_rows, padded = pieces_ref.shape
    width = across_ref.shape[2]
    for row in range(0, band_rows, 8):
        rows = slice(row, row + 8)
        totals = [None] * 4
        passed = None
        for tile in range(tiles):
            parts = [pieces_ref[tile, channel, rows, :].astype(jnp.float32) for channel in range(4)]
            if tile == 0:
                totals = parts[:3]
                passed = 1.0 - parts[3]
            else:
                totals = [total + passed * part for total, part in zip(totals, parts[:3])]
                passed = passed - passed * parts[3]
        totals = totals[:3] + [1.0 - passed]
        shifts = jnp.broadcast_to(shifts_ref[rows, :], (8, width))
        results = [jnp.zeros((8, width), jnp.float32)] * 4
        for offset in range(-RIM, RIM + 1):
            factor = weight_of(offset - shifts)
            for channel in range(4):
                moved = pltpu.roll(totals[channel], (-offset) % padded, 1)[:, :width]
                results[channel] = results[channel] + factor * moved
        for channel in range(4):
            across_ref[channel, rows, :] = results[channel]
    for channel in range(4):
        top_ref[channel * RIM : (channel + 1) * RIM, :] = across_ref[channel, 0:RIM, :]
        bottom_ref[channel * RIM : (channel + 1) * RIM, :] = across_ref[
            channel, band_rows - RIM : band_rows, :
        ]


def warp_columns(pieces, shifts, width):
    _, _, band_rows, _ = pieces.shape
    rim = jax.ShapeDtypeStruct((4 * RIM, width), jnp.float32)
    return pl.pallas_call(
        across_kernel,
        out_shape=(jax.ShapeDtypeStruct((4, band_rows, width), jnp.float32), rim, rim),
        compiler_params=pltpu.CompilerParams(vmem_limit_bytes=VMEM_LIMIT),
    )(pieces, shifts)


def final_kernel(across_ref, low_ref, high_ref, shifts_ref, final_ref, extended):
    _, band_rows, width = across_ref.shape
    for channel in range(4):
        extended[channel, 16 : 16 + band_rows, :] = across_ref[channel]
        rim = slice(channel * RIM, (channel + 1) * RIM)
        extended[channel, 16 - RIM : 16, :] = low_ref[rim, :]
        extended[channel, 16 + band_rows : 16 + band_rows + RIM, :] = high_ref[rim, :]
    for lane in range(0, width, 128):
        lanes = slice(lane, lane + 128)
        shifts = jnp.broadcast_to(shifts_ref[:, lanes], (8, 128))
        factors = [weight_of(offset - shifts) for offset in range(-RIM, RIM + 1)]
        for channel in range(4):
            for row in range(0, band_rows, 8):
                result = jnp.zeros((8, 128), jnp.float32)
                for offset in range(-RIM, RIM + 1):
                    start = 16 + row + offset
                    result = result + factors[offset + RIM] * extended[
                        channel, start : start + 8, lanes
                    ]
                final_ref[channel, row : row + 8, lanes] = result


def warp_rows_of(across, low, high, shifts):
    _, band_rows, width = across.shape
    return pl.pallas_call(
        final_kernel,
        out_shape=jax.ShapeDtypeStruct(across.shape, jnp.float32),
        scratch_shapes=[pltpu.VMEM((4, band_rows + 32, width), jnp.float32)],
        compiler_params=pltpu.CompilerParams(vmem_limit_bytes=VMEM_LIMIT),
    )(across, low, high, shifts)


def over_front(front_part, back_part):
    return front_part + (1.0 - front_part[:, 3:4]) * back_part


def neighbours(axis):
    count = lax.axis_size(axis)
    forward = [(i, i + 1) for i in range(count - 1)]
    return forward, [(target, source) for source, target in forward]


def per_device(volume, shear_rows, shear_cols, warp_cols, warp_rows):
    band_rows = volume.shape[2]
    columns = volume.shape[3]
    tiles = lax.axis_size("depth")
    width = columns // tiles
    core = lax.axis_index("depth") % 2
    forward, backward = neighbours("rows")
    slices = volume.shape[1]
    most = -(-RIM * slices // 8)
    sizes = [size for size in SIZES if size < most] + [most]
    earlier = jnp.arange(slices)[None, :] <= jnp.arange(slices)[:, None]
    reach = jnp.maximum(
        jnp.sum(jnp.where(earlier, rows_from_high(shear_rows)[None, :], 0), 1),
        jnp.sum(jnp.where(earlier, rows_from_low(shear_rows)[None, :], 0), 1),
    )
    needed = jnp.maximum(
        jnp.sum(rows_from_high(shear_rows)), jnp.sum(rows_from_low(shear_rows))
    )
    choice = sum((needed > 8 * size).astype(jnp.int32) for size in sizes[:-1])

    def with_groups(groups):
        early = groups * 3 // 7
        late = groups - early

        def branch(volume, shear_rows, shear_cols, reach):
            middle = jnp.minimum(jnp.sum((reach <= 8 * early).astype(jnp.int32)), slices - 1)
            begin, end = jnp.zeros_like(middle), jnp.full_like(middle, slices)
            up_first, down_first = pack_halo(volume, shear_rows, 0, early)
            up_second, down_second = pack_halo(volume, shear_rows, early, late)
            high_first = lax.ppermute(up_first, "rows", backward)
            low_first = lax.ppermute(down_first, "rows", forward)
            high_second = lax.ppermute(up_second, "rows", backward)
            low_second = lax.ppermute(down_second, "rows", forward)
            (total,) = shear_part(
                "front", jnp.stack([begin, middle]), volume, shear_rows, shear_cols,
                (low_first, high_first), None, tiles,
            )
            return shear_part(
                "back", jnp.stack([middle, end, core]), volume, shear_rows, shear_cols,
                (low_first, low_second, high_first, high_second), total, tiles,
            )

        return branch

    kept, sent = lax.switch(
        choice, [with_groups(groups) for groups in sizes], volume, shear_rows, shear_cols, reach
    )
    received = lax.ppermute(sent, "depth", [(i, i ^ 1) for i in range(tiles)])
    merged = over_front(
        jnp.where(core == 0, kept, received).astype(jnp.float32),
        jnp.where(core == 0, received, kept).astype(jnp.float32),
    ).astype(jnp.bfloat16)
    pieces = lax.all_to_all(
        merged, "depth", 0, 0, tiled=True,
        axis_index_groups=[list(range(first, tiles, 2)) for first in range(2)],
    )
    row_start = lax.axis_index("rows") * band_rows
    row_shifts = lax.dynamic_slice_in_dim(warp_cols, row_start, band_rows, 0)
    across, top, bottom = warp_columns(pieces, row_shifts[:, None], width)
    below = lax.ppermute(bottom, "rows", forward)
    above = lax.ppermute(top, "rows", backward)
    return warp_rows_of(across, below, above, warp_rows[None, :])


def solution(mesh):
    return jax.shard_map(
        per_device,
        mesh=mesh,
        in_specs=(P(None, "depth", "rows", None), P("depth"), P("depth"), P(), P("depth")),
        out_specs=P(None, "rows", "depth"),
        check_vma=False,
    )
```
